32 devices in a mesh: section: 8 (over y, x, core), fsdp: 4 (over z).
Axes of the slice: x: 2, y: 2, z: 4, core: 2. Of those that a mesh axis runs over, the one named last changes fastest.
Arguments:
- layer_input: bfloat16 [8, 512, 4096], P('section', 'fsdp'), may hold values from -6 to 6
- next_cot: bfloat16 [8, 512, 512], P('section', 'fsdp'), may hold values from -6 to 6
- w_value: bfloat16 [8, 4096, 512], P('section', 'fsdp'), may hold values from -0.25 to 0.25
- micro_ids: int32 [8, 4], P('section', 'fsdp'), may hold values from 0 to 1
Outputs:
- grad_input: bfloat16 [8, 512, 4096], P('section', 'fsdp')
- grad_sum: float32 [8, 4096, 512], P('section', 'fsdp')
- grad_square: float32 [8, 4096, 512], P('section', 'fsdp')
The draws below stay inside these ranges and needn't reach their ends.
All inputs are finite; a program needn't handle non-finite values.
Results may differ from the reference program's by a relative error of at most 0.0037.
Values may be sent and summed in bfloat16 or wider, within the bound.
A program may use at most 64 MiB of HBM per device.

```python
import jax
import jax.numpy as jnp
from jax import lax

D = 4096
MICRO = 2
TOK_DEV = 128
KVC = 512
TOKF = 512
N_SECTION = 8
N_FSDP = 4


def plant(drawn, rng, low, top_value):
    extent = drawn.shape
    place = [jax.random.randint(jax.random.fold_in(rng, axis), (), 0, extent[axis]) for axis in range(len(extent))]
    drawn = drawn.at[tuple(place)].set(low)
    longest = extent.index(max(extent))
    place[longest] = (place[longest] + 1) % extent[longest]
    return drawn.at[tuple(place)].set(top_value)


def raised(values, own_key, source, target, parts, factor):
    owner, partner = [(jnp.arange(values.shape[position]) // (values.shape[position] // parts)).reshape([-1 if axis == position else 1 for axis in range(values.ndim)]) for position in (source, target)]
    chosen = jax.random.permutation(own_key, parts)[partner]
    strong = (owner == chosen) | (owner == (partner + parts // 2) % parts)
    return jnp.where(strong, factor * values, values)


def steps_of(key, extent, cuts, smallest, top_value):
    gain, own = 1.0, jax.random.fold_in(key, 6)
    for position, blocks in cuts:
        heights = jnp.exp(jax.random.uniform(jax.random.fold_in(own, position), (blocks,), jnp.float32, smallest / len(cuts), top_value / len(cuts)))
        gain = gain * jnp.repeat(heights, extent[position] // blocks).reshape([-1 if axis == position else 1 for axis in range(len(extent))])
    return gain


def bell_draw(stream_key, extent, scale, most, shards=(), kind=jnp.bfloat16):
    level = steps_of(stream_key, extent, shards, -0.22, 0.18) if shards else 1.0
    entries = jax.random.normal(stream_key, extent, jnp.float32) * scale * level
    return jnp.minimum(jnp.maximum(entries, -most), most).astype(kind)


def bell_draw_with(key, extent, scale, most, cuts, heavy, kind=jnp.bfloat16):
    entries = scale * jax.random.normal(key, extent, jnp.float32)
    if cuts:
        entries = entries * steps_of(key, extent, cuts, -0.22, 0.18)
    return jnp.clip(raised(entries, jax.random.fold_in(key, 3), *heavy), -most, most).astype(kind)


def setup_inputs(seed: int = 0) -> dict:
    arg_keys = jax.random.split(jax.random.key(seed), 5)
    return {
        "layer_input": bell_draw_with(arg_keys[0], (N_SECTION, TOKF, D), 1.0, 6.0, ((0, 8), (1, 4)), (1, 2, 4, 2.0)),
        "next_cot": bell_draw(arg_keys[1], (N_SECTION, TOKF, KVC), 1.0, 6.0, ((0, 8), (1, 4))),
        "w_value": bell_draw(arg_keys[2], (N_SECTION, D, KVC), KVC ** -0.5, 0.25, ((0, 8), (1, 4))),
        "micro_ids": plant(jax.random.randint(arg_keys[3], (N_SECTION, N_FSDP), 0, MICRO), jax.random.fold_in(arg_keys[3], 1), 0, MICRO - 1).astype(jnp.int32),
    }


def one_section(operands):
    inputs_section, cot_section, weight_section, micro_section = operands
    grad_in = jnp.dot(cot_section, weight_section.T, preferred_element_type=jnp.float32).astype(jnp.bfloat16)
    blocks_in = inputs_section.reshape(N_FSDP, TOK_DEV, D).astype(jnp.float32)
    blocks_cot = cot_section.reshape(N_FSDP, TOK_DEV, KVC).astype(jnp.float32)
    partial_value = jnp.einsum('ftd,ftc->fdc', blocks_in, blocks_cot) * (1.0 / TOK_DEV)
    partial_value = lax.optimization_barrier(partial_value.astype(jnp.bfloat16)).astype(jnp.float32)
    onehot = (micro_section[:, None] == jnp.arange(MICRO, dtype=jnp.int32)[None, :]).astype(jnp.float32)
    per_micro = jnp.einsum('fm,fdc->mdc', onehot, partial_value)
    return grad_in, jnp.sum(per_micro, axis=0), jnp.sum(per_micro * per_micro, axis=0)


def reference(layer_input, next_cot, w_value, micro_ids):
    incoming = jnp.roll(next_cot, -1, axis=0)
    grad_input, grad_sum, grad_square = lax.map(one_section, (layer_input, incoming, w_value, micro_ids))
    return (grad_input, grad_sum, grad_square)
```

```python
import functools

import jax
import jax.numpy as jnp
from jax import lax
from jax.experimental import pallas as pl
from jax.experimental.pallas import tpu as pltpu
from jax.sharding import PartitionSpec as P

MICRO = 2
MESH = pl.DeviceIdType.MESH
PIECES = 4
HEAD = 3
FAR = 1
BETWEEN = 2


def kernel(
    n, ns, li, cot, w, mid, gi, gs, gq,
    inc, lix, gis, ids, wv,
    perm_s, perm_r, right_s, left_s, cot_r, li_s, li_r, gi_s, gi_r, id_s, id_r, own_s,
    above, below,
):
    f = lax.axis_index("fsdp")
    s = lax.axis_index("section")
    behind = lax.rem(s + ns - 1, ns)
    ahead = lax.rem(s + 1, ns)
    tokens, share = lix.shape[1], lix.shape[2]
    columns = inc.shape[2]

    def share_of(ref, part, rows=slice(None)):
        return ref.at[rows, pl.ds(pl.multiple_of(part * share, share), share)]

    def li_copy(target, rows=slice(None)):
        return pltpu.make_async_remote_copy(
            src_ref=share_of(li, target, rows),
            dst_ref=lix.at[f, rows],
            send_sem=li_s.at[target],
            recv_sem=li_r.at[f],
            device_id={"fsdp": target},
            device_id_type=MESH,
        )

    def cot_copy(block, target, sem):
        return pltpu.make_async_remote_copy(
            src_ref=inc.at[block],
            dst_ref=inc.at[block],
            send_sem=sem.at[block],
            recv_sem=cot_r.at[block],
            device_id={"fsdp": target},
            device_id_type=MESH,
        )

    def gi_copy(target):
        return pltpu.make_async_remote_copy(
            src_ref=gis.at[target],
            dst_ref=share_of(gi, f),
            send_sem=gi_s.at[target],
            recv_sem=gi_r.at[f],
            device_id={"fsdp": target},
            device_id_type=MESH,
        )

    def id_copy(target, owner):
        return pltpu.make_async_remote_copy(
            src_ref=ids.at[owner],
            dst_ref=ids.at[owner],
            send_sem=id_s.at[target],
            recv_sem=id_r.at[owner],
            device_id={"fsdp": target},
            device_id_type=MESH,
        )

    permute = pltpu.make_async_remote_copy(
        src_ref=cot,
        dst_ref=inc.at[f],
        send_sem=perm_s,
        recv_sem=perm_r,
        device_id={"section": behind},
        device_id_type=MESH,
    )
    weights = pltpu.make_async_copy(w, wv, own_s.at[0])
    own_li = pltpu.make_async_copy(share_of(li, f), lix.at[f], own_s.at[1])

    def tell(sem, target, cond):
        @pl.when(cond)
        def _():
            pl.semaphore_signal(sem, inc=1, device_id={"fsdp": target}, device_id_type=MESH)

    barrier = pltpu.get_barrier_semaphore()
    tell(barrier, f + 1, f < n - 1)
    pl.semaphore_signal(barrier, inc=1, device_id={"section": ahead}, device_id_type=MESH)
    pl.semaphore_wait(barrier, 1 + (f > 0).astype(jnp.int32))

    pieces = PIECES
    rows = tokens // pieces

    half = n // 2
    head = min(HEAD, pieces)
    total = half * pieces

    def crossing(index):
        owner, piece = index // pieces, index % pieces
        window = pl.ds(piece * rows, rows)
        first = owner == half - 1 and piece < head

        @pl.when((f < half - 1) if first else (f < half))
        def _():
            li_copy(n - 1 - owner, window).start()

        @pl.when((f > half) if first else (f >= half))
        def _():
            li_copy(owner, window).start()

    def forward(step):
        @pl.when((f - step >= 0) & (f < n - 1))
        def _():
            cot_copy(f - step, f + 1, right_s).start()

        @pl.when((f + step < n) & (f > 0))
        def _():
            cot_copy(f + step, f - 1, left_s).start()

    def arrived(step):
        @pl.when(f - step >= 0)
        def _():
            cot_copy(f - step, f, right_s).wait_recv()

        @pl.when(f + step < n)
        def _():
            cot_copy(f + step, f, left_s).wait_recv()

    tell(above.at[1], f - 1, f > 0)
    permute.start()

    @pl.when(f == half)
    def _():
        li_copy(half - 1, pl.ds(0, head * rows)).start()

    @pl.when(f < n - 1)
    def _():
        pl.semaphore_wait(above.at[1], 1)

    @pl.when(f == half - 1)
    def _():
        li_copy(half, pl.ds(0, head * rows)).start()

    if n > 2:
        tell(above.at[2], f - 1, (f > 0) & (f + 1 < n))
        tell(below.at[2], f + 1, (f < n - 1) & (f - 1 >= 0))
    weights.start()
    own_li.start()
    ids[f] = jnp.full(ids.shape[1:], mid[0, 0], jnp.int32)
    for d in range(2, n):
        @pl.when(f + d < n)
        def _():
            pl.semaphore_wait(above.at[d], 1)

        @pl.when(f - d >= 0)
        def _():
            pl.semaphore_wait(below.at[d], 1)

        if d + 1 < n:
            tell(above.at[d + 1], f - 1, (f > 0) & (f + d < n))
            tell(below.at[d + 1], f + 1, (f < n - 1) & (f - d >= 0))

    issued = 0
    for index in range(issued, FAR):
        crossing(index)
    issued = FAR
    permute.wait_recv()
    forward(0)
    for step in range(1, n):
        target = lax.rem(f + step, n)
        id_copy(target, f).start()
    for step in range(1, n - 1):
        upto = min(total, issued + BETWEEN)
        for index in range(issued, upto):
            crossing(index)
        issued = upto
        arrived(step)
        forward(step)
    for index in range(issued, total):
        crossing(index)
    for distance in range(n - 1, 0, -1):
        @pl.when((f + distance < n) & ((f + distance < half) | (f >= half)))
        def _():
            li_copy(f + distance).start()

        @pl.when((f - distance >= 0) & ((f < half) | (f - distance >= half)))
        def _():
            li_copy(f - distance).start()

    weights.wait()

    def input_block(block):
        gis[block] = lax.dot_general(
            inc[block], wv[...], (((1,), (1,)), ((), ())), preferred_element_type=jnp.float32
        ).astype(gis.dtype)

    arrived(n - 1)

    def input_blocks(block, carry):
        input_block(block)
        return carry

    lax.fori_loop(0, n, input_blocks, 0)
    own_gi = pltpu.make_async_copy(gis.at[f], share_of(gi, f), own_s.at[2])
    own_gi.start()
    for d in range(n - 1, 0, -1):
        @pl.when(f + d < n)
        def _():
            gi_copy(f + d).start()

        @pl.when(f - d >= 0)
        def _():
            gi_copy(f - d).start()

    own_li.wait()

    def others(action):
        def run(step, carry):
            action(lax.rem(f + step, n))
            return carry

        lax.fori_loop(1, n, run, 0)

    def li_wait(peer):
        pltpu.make_async_remote_copy(
            src_ref=share_of(li, peer),
            dst_ref=lix.at[peer],
            send_sem=li_s.at[peer],
            recv_sem=li_r.at[peer],
            device_id={"fsdp": peer},
            device_id_type=MESH,
        ).wait()
        id_copy(peer, peer).wait()

    others(li_wait)

    inverse = 1.0 / tokens
    tile = 128

    def weight_rows(index, carry):
        start = pl.multiple_of(index * tile, tile)
        micro = [jnp.zeros((tile, columns), jnp.float32) for _ in range(MICRO)]
        for block in range(n):
            product = lax.dot_general(
                lix[block, :, pl.ds(start, tile)],
                inc[block],
                (((0,), (0,)), ((), ())),
                preferred_element_type=jnp.float32,
            )
            product = (product * inverse).astype(jnp.bfloat16).astype(jnp.float32)
            owner = jnp.broadcast_to(ids[block][:1, :1], product.shape)
            for m in range(MICRO):
                micro[m] = micro[m] + jnp.where(owner == m, product, 0.0)
        total = micro[0]
        square = micro[0] * micro[0]
        for m in range(1, MICRO):
            total = total + micro[m]
            square = square + micro[m] * micro[m]
        gs[pl.ds(start, tile), :] = total
        gq[pl.ds(start, tile), :] = square
        return carry

    lax.fori_loop(0, share // tile, weight_rows, 0)

    own_gi.wait()
    permute.wait_send()
    for step in range(n - 1):
        @pl.when((f - step >= 0) & (f < n - 1))
        def _():
            cot_copy(f - step, f + 1, right_s).wait_send()

        @pl.when((f + step < n) & (f > 0))
        def _():
            cot_copy(f + step, f - 1, left_s).wait_send()

    def gi_wait(peer):
        pltpu.make_async_remote_copy(
            src_ref=gis.at[peer],
            dst_ref=share_of(gi, peer),
            send_sem=gi_s.at[peer],
            recv_sem=gi_r.at[peer],
            device_id={"fsdp": peer},
            device_id_type=MESH,
        ).wait()

    others(gi_wait)


def settle_kernel(cuts, *refs):
    count = len(refs) // 2
    sems = refs[-1]
    copies = []
    for index in range(count):
        source, target = refs[index], refs[count + index]
        rows = source.shape[0] // cuts
        for cut in range(cuts):
            window = pl.ds(cut * rows, rows)
            copies.append(
                pltpu.make_async_copy(source.at[window], target.at[window], sems.at[index, cut])
            )
    for copy in copies:
        copy.start()
    for copy in copies:
        copy.wait()


def settle(*arrays):
    cuts = 1
    return pl.pallas_call(
        functools.partial(settle_kernel, cuts),
        out_shape=tuple(jax.ShapeDtypeStruct(a.shape, a.dtype) for a in arrays),
        in_specs=[pl.BlockSpec(memory_space=pl.ANY)] * len(arrays),
        out_specs=tuple(pl.BlockSpec(memory_space=pltpu.HBM) for _ in arrays),
        scratch_shapes=[pltpu.SemaphoreType.DMA((len(arrays), cuts))],
        compiler_params=pltpu.CompilerParams(vmem_limit_bytes=4 * 2**20),
    )(*[pltpu.with_memory_space_constraint(a, pltpu.VMEM) for a in arrays])


def body(layer_input, next_cot, w_value, micro_ids):
    n = lax.axis_size("fsdp")
    ns = lax.axis_size("section")
    tokens, width = layer_input.shape[1:]
    share, columns = w_value.shape[1:]
    anywhere = pl.BlockSpec(memory_space=pltpu.HBM)
    dma = pltpu.SemaphoreType.DMA
    stay = functools.partial(pltpu.with_memory_space_constraint, memory_space=pltpu.HBM)
    arrays = pl.pallas_call(
        functools.partial(kernel, n, ns),
        out_shape=(
            jax.ShapeDtypeStruct((tokens, width), jnp.bfloat16),
            jax.ShapeDtypeStruct((share, columns), jnp.float32),
            jax.ShapeDtypeStruct((share, columns), jnp.float32),
        ),
        in_specs=[anywhere, anywhere, anywhere, pl.BlockSpec(memory_space=pltpu.SMEM)],
        out_specs=OUT_SPECS,
        scratch_shapes=[
            pltpu.VMEM((n, tokens, columns), jnp.bfloat16),
            pltpu.VMEM((n, tokens, share), jnp.bfloat16),
            pltpu.VMEM((n, tokens, share), jnp.bfloat16),
            pltpu.VMEM((n, 8, 128), jnp.int32),
            pltpu.VMEM((share, columns), jnp.bfloat16),
            dma, dma, dma((n,)), dma((n,)), dma((n,)), dma((n,)), dma((n,)),
            dma((n,)), dma((n,)), dma((n,)), dma((n,)), dma((3,)),
            pltpu.SemaphoreType.REGULAR((n,)), pltpu.SemaphoreType.REGULAR((n,)),
        ],
        compiler_params=pltpu.CompilerParams(
            collective_id=0, has_side_effects=True, vmem_limit_bytes=40 * 2**20
        ),
    )(stay(layer_input[0]), stay(next_cot[0]), stay(w_value[0]), micro_ids)
    grad_input, grad_sum, grad_square = settle(*arrays)
    return (grad_input[None], grad_sum[None], grad_square[None])


OUT_SPECS = (
    pl.BlockSpec(memory_space=pl.ANY),
    pl.BlockSpec(memory_space=pltpu.VMEM),
    pl.BlockSpec(memory_space=pltpu.VMEM),
)


def solution(mesh):
    spec = P("section", "fsdp", None)
    return jax.shard_map(
        body,
        mesh=mesh,
        in_specs=(spec, spec, spec, P("section", "fsdp")),
        out_specs=(spec, spec, spec),
        check_vma=False,
    )
```

```python
import functools

import jax
import jax.numpy as jnp
from jax import lax
from jax.experimental import pallas as pl
from jax.experimental.pallas import tpu as pltpu
from jax.sharding import PartitionSpec as P

MICRO = 2
MESH = pl.DeviceIdType.MESH
PIECES = 4
HEAD = 3
FAR = 0
BETWEEN = 2


def kernel(
    n, ns, li, cot, w, mid, gi, gs, gq,
    inc, lix, gis, ids, wv,
    perm_s, perm_r, right_s, left_s, cot_r, li_s, li_r, gi_s, gi_r, id_s, id_r, own_s,
    above, below, pair,
):
    f = lax.axis_index("fsdp")
    s = lax.axis_index("section")
    behind = lax.rem(s + ns - 1, ns)
    ahead = lax.rem(s + 1, ns)
    tokens, share = lix.shape[1], lix.shape[2]
    columns = inc.shape[2]

    def share_of(ref, part, rows=slice(None)):
        return ref.at[rows, pl.ds(pl.multiple_of(part * share, share), share)]

    def li_copy(target, rows=slice(None)):
        return pltpu.make_async_remote_copy(
            src_ref=share_of(li, target, rows),
            dst_ref=lix.at[f, rows],
            send_sem=li_s.at[target],
            recv_sem=li_r.at[f],
            device_id={"fsdp": target},
            device_id_type=MESH,
        )

    def cot_copy(block, target, sem):
        return pltpu.make_async_remote_copy(
            src_ref=inc.at[block],
            dst_ref=inc.at[block],
            send_sem=sem.at[block],
            recv_sem=cot_r.at[block],
            device_id={"fsdp": target},
            device_id_type=MESH,
        )

    def gi_copy(target):
        return pltpu.make_async_remote_copy(
            src_ref=gis.at[target],
            dst_ref=share_of(gi, f),
            send_sem=gi_s.at[target],
            recv_sem=gi_r.at[f],
            device_id={"fsdp": target},
            device_id_type=MESH,
        )

    def id_copy(target, owner):
        return pltpu.make_async_remote_copy(
            src_ref=ids.at[owner],
            dst_ref=ids.at[owner],
            send_sem=id_s.at[target],
            recv_sem=id_r.at[owner],
            device_id={"fsdp": target},
            device_id_type=MESH,
        )

    permute = pltpu.make_async_remote_copy(
        src_ref=cot,
        dst_ref=inc.at[f],
        send_sem=perm_s,
        recv_sem=perm_r,
        device_id={"section": behind},
        device_id_type=MESH,
    )
    weights = pltpu.make_async_copy(w, wv, own_s.at[0])
    own_li = pltpu.make_async_copy(share_of(li, f), lix.at[f], own_s.at[1])

    def tell(sem, target, cond):
        @pl.when(cond)
        def _():
            pl.semaphore_signal(sem, inc=1, device_id={"fsdp": target}, device_id_type=MESH)

    barrier = pltpu.get_barrier_semaphore()
    tell(barrier, f + 1, f < n - 1)

    @pl.when(s < ns - 1)
    def _():
        pl.semaphore_signal(barrier, inc=1, device_id={"section": ahead}, device_id_type=MESH)

    @pl.when(s == 0)
    def _():
        pl.semaphore_signal(barrier, inc=1, device_id={"section": behind}, device_id_type=MESH)

    greetings = (f > 0).astype(jnp.int32) + (s > 0).astype(jnp.int32) + (s == ns - 1).astype(jnp.int32)

    @pl.when(greetings > 0)
    def _():
        pl.semaphore_wait(barrier, greetings)

    @pl.when(s == ns - 1)
    def _():
        pl.semaphore_signal(pair, inc=1, device_id={"section": ahead}, device_id_type=MESH)

    pieces = PIECES
    rows = tokens // pieces

    half = n // 2
    head = min(HEAD, pieces)
    total = half * pieces

    def crossing(index):
        owner, piece = index // pieces, index % pieces
        window = pl.ds(piece * rows, rows)
        first = owner == half - 1 and piece < head

        @pl.when((f < half - 1) if first else (f < half))
        def _():
            li_copy(n - 1 - owner, window).start()

        @pl.when((f > half) if first else (f >= half))
        def _():
            li_copy(owner, window).start()

    def forward(step):
        @pl.when((f - step >= 0) & (f < n - 1))
        def _():
            cot_copy(f - step, f + 1, right_s).start()

        @pl.when((f + step < n) & (f > 0))
        def _():
            cot_copy(f + step, f - 1, left_s).start()

    def arrived(step):
        @pl.when(f - step >= 0)
        def _():
            cot_copy(f - step, f, right_s).wait_recv()

        @pl.when(f + step < n)
        def _():
            cot_copy(f + step, f, left_s).wait_recv()

    tell(above.at[1], f - 1, f > 0)

    @pl.when(s > 0)
    def _():
        permute.start()

    @pl.when(f == half)
    def _():
        li_copy(half - 1, pl.ds(0, head * rows)).start()

    @pl.when(f < n - 1)
    def _():
        pl.semaphore_wait(above.at[1], 1)

    @pl.when(f == half - 1)
    def _():
        li_copy(half, pl.ds(0, head * rows)).start()

    if n > 2:
        tell(above.at[2], f - 1, (f > 0) & (f + 1 < n))
        tell(below.at[2], f + 1, (f < n - 1) & (f - 1 >= 0))
    weights.start()
    own_li.start()
    ids[f] = jnp.full(ids.shape[1:], mid[0, 0], jnp.int32)
    for d in range(2, n):
        @pl.when(f + d < n)
        def _():
            pl.semaphore_wait(above.at[d], 1)

        @pl.when(f - d >= 0)
        def _():
            pl.semaphore_wait(below.at[d], 1)

        if d + 1 < n:
            tell(above.at[d + 1], f - 1, (f > 0) & (f + d < n))
            tell(below.at[d + 1], f + 1, (f < n - 1) & (f - d >= 0))

    @pl.when(s == 0)
    def _():
        pl.semaphore_wait(pair, 1)
        permute.start()

    issued = FAR
    for index in range(issued):
        crossing(index)
    permute.wait_recv()
    forward(0)
    for step in range(1, n):
        target = lax.rem(f + step, n)
        id_copy(target, f).start()
    for step in range(1, n - 1):
        upto = min(total, issued + BETWEEN)
        for index in range(issued, upto):
            crossing(index)
        issued = upto
        arrived(step)
        forward(step)
    for index in range(issued, total):
        crossing(index)
    for distance in range(n - 1, 0, -1):
        @pl.when((f + distance < n) & ((f + distance < half) | (f >= half)))
        def _():
            li_copy(f + distance).start()

        @pl.when((f - distance >= 0) & ((f < half) | (f - distance >= half)))
        def _():
            li_copy(f - distance).start()

    weights.wait()

    def input_block(block):
        gis[block] = lax.dot_general(
            inc[block], wv[...], (((1,), (1,)), ((), ())), preferred_element_type=jnp.float32
        ).astype(gis.dtype)

    arrived(n - 1)

    def input_blocks(block, carry):
        input_block(block)
        return carry

    lax.fori_loop(0, n, input_blocks, 0)
    own_gi = pltpu.make_async_copy(gis.at[f], share_of(gi, f), own_s.at[2])
    own_gi.start()
    for d in range(n - 1, 0, -1):
        @pl.when(f + d < n)
        def _():
            gi_copy(f + d).start()

        @pl.when(f - d >= 0)
        def _():
            gi_copy(f - d).start()

    own_li.wait()

    def others(action):
        def run(step, carry):
            action(lax.rem(f + step, n))
            return carry

        lax.fori_loop(1, n, run, 0)

    def li_wait(peer):
        pltpu.make_async_remote_copy(
            src_ref=share_of(li, peer),
            dst_ref=lix.at[peer],
            send_sem=li_s.at[peer],
            recv_sem=li_r.at[peer],
            device_id={"fsdp": peer},
            device_id_type=MESH,
        ).wait()
        id_copy(peer, peer).wait()

    others(li_wait)

    inverse = 1.0 / tokens
    tile = 128

    def weight_rows(index, carry):
        start = pl.multiple_of(index * tile, tile)
        micro = [jnp.zeros((tile, columns), jnp.float32) for _ in range(MICRO)]
        for block in range(n):
            product = lax.dot_general(
                lix[block, :, pl.ds(start, tile)],
                inc[block],
                (((0,), (0,)), ((), ())),
                preferred_element_type=jnp.float32,
            )
            product = (product * inverse).astype(jnp.bfloat16).astype(jnp.float32)
            owner = jnp.broadcast_to(ids[block][:1, :1], product.shape)
            for m in range(MICRO):
                micro[m] = micro[m] + jnp.where(owner == m, product, 0.0)
        total = micro[0]
        square = micro[0] * micro[0]
        for m in range(1, MICRO):
            total = total + micro[m]
            square = square + micro[m] * micro[m]
        gs[pl.ds(start, tile), :] = total
        gq[pl.ds(start, tile), :] = square
        return carry

    lax.fori_loop(0, share // tile, weight_rows, 0)

    own_gi.wait()
    permute.wait_send()
    for step in range(n - 1):
        @pl.when((f - step >= 0) & (f < n - 1))
        def _():
            cot_copy(f - step, f + 1, right_s).wait_send()

        @pl.when((f + step < n) & (f > 0))
        def _():
            cot_copy(f + step, f - 1, left_s).wait_send()

    def gi_wait(peer):
        pltpu.make_async_remote_copy(
            src_ref=gis.at[peer],
            dst_ref=share_of(gi, peer),
            send_sem=gi_s.at[peer],
            recv_sem=gi_r.at[peer],
            device_id={"fsdp": peer},
            device_id_type=MESH,
        ).wait()

    others(gi_wait)


def settle_kernel(cuts, *refs):
    count = len(refs) // 2
    sems = refs[-1]
    copies = []
    for index in range(count):
        source, target = refs[index], refs[count + index]
        rows = source.shape[0] // cuts
        for cut in range(cuts):
            window = pl.ds(cut * rows, rows)
            copies.append(
                pltpu.make_async_copy(source.at[window], target.at[window], sems.at[index, cut])
            )
    for copy in copies:
        copy.start()
    for copy in copies:
        copy.wait()


def settle(*arrays):
    cuts = 1
    return pl.pallas_call(
        functools.partial(settle_kernel, cuts),
        out_shape=tuple(jax.ShapeDtypeStruct(a.shape, a.dtype) for a in arrays),
        in_specs=[pl.BlockSpec(memory_space=pl.ANY)] * len(arrays),
        out_specs=tuple(pl.BlockSpec(memory_space=pltpu.HBM) for _ in arrays),
        scratch_shapes=[pltpu.SemaphoreType.DMA((len(arrays), cuts))],
        compiler_params=pltpu.CompilerParams(vmem_limit_bytes=4 * 2**20),
    )(*[pltpu.with_memory_space_constraint(a, pltpu.VMEM) for a in arrays])


def body(layer_input, next_cot, w_value, micro_ids):
    n = lax.axis_size("fsdp")
    ns = lax.axis_size("section")
    tokens, width = layer_input.shape[1:]
    share, columns = w_value.shape[1:]
    anywhere = pl.BlockSpec(memory_space=pltpu.HBM)
    dma = pltpu.SemaphoreType.DMA
    stay = functools.partial(pltpu.with_memory_space_constraint, memory_space=pltpu.HBM)
    arrays = pl.pallas_call(
        functools.partial(kernel, n, ns),
        out_shape=(
            jax.ShapeDtypeStruct((tokens, width), jnp.bfloat16),
            jax.ShapeDtypeStruct((share, columns), jnp.float32),
            jax.ShapeDtypeStruct((share, columns), jnp.float32),
        ),
        in_specs=[anywhere, anywhere, anywhere, pl.BlockSpec(memory_space=pltpu.SMEM)],
        out_specs=OUT_SPECS,
        scratch_shapes=[
            pltpu.VMEM((n, tokens, columns), jnp.bfloat16),
            pltpu.VMEM((n, tokens, share), jnp.bfloat16),
            pltpu.VMEM((n, tokens, share), jnp.bfloat16),
            pltpu.VMEM((n, 8, 128), jnp.int32),
            pltpu.VMEM((share, columns), jnp.bfloat16),
            dma, dma, dma((n,)), dma((n,)), dma((n,)), dma((n,)), dma((n,)),
            dma((n,)), dma((n,)), dma((n,)), dma((n,)), dma((3,)),
            pltpu.SemaphoreType.REGULAR((n,)), pltpu.SemaphoreType.REGULAR((n,)), pltpu.SemaphoreType.REGULAR,
        ],
        compiler_params=pltpu.CompilerParams(
            collective_id=0, has_side_effects=True, vmem_limit_bytes=40 * 2**20
        ),
    )(stay(layer_input[0]), stay(next_cot[0]), stay(w_value[0]), micro_ids)
    grad_input, grad_sum, grad_square = settle(*arrays)
    return (grad_input[None], grad_sum[None], grad_square[None])


OUT_SPECS = (
    pl.BlockSpec(memory_space=pl.ANY),
    pl.BlockSpec(memory_space=pltpu.VMEM),
    pl.BlockSpec(memory_space=pltpu.VMEM),
)


def solution(mesh):
    spec = P("section", "fsdp", None)
    return jax.shard_map(
        body,
        mesh=mesh,
        in_specs=(spec, spec, spec, P("section", "fsdp")),
        out_specs=(spec, spec, spec),
        check_vma=False,
    )
```

```python
import functools

import jax
import jax.numpy as jnp
from jax import lax
from jax.experimental import pallas as pl
from jax.experimental.pallas import tpu as pltpu
from jax.sharding import PartitionSpec as P

MICRO = 2
MESH = pl.DeviceIdType.MESH
PIECES = 4
HEAD = (3, 2, 2, 3)
BETWEEN = (2, 1, 2, 2)
TILE = 256
AT_ONCE = 1
INNER = 4


def tell(sem, target, cond):
    @pl.when(cond)
    def _():
        pl.semaphore_signal(sem, inc=1, device_id={"fsdp": target}, device_id_type=MESH)


def share_of(ref, part, share, rows=slice(None)):
    return ref.at[rows, pl.ds(pl.multiple_of(part * share, share), share)]


def gi_copy(peer, owner, gis, gi, gi_s, gi_r, rows=slice(None)):
    return pltpu.make_async_remote_copy(
        src_ref=gis.at[peer, rows],
        dst_ref=share_of(gi, owner, gis.shape[2], rows),
        send_sem=gi_s.at[peer],
        recv_sem=gi_r.at[owner],
        device_id={"fsdp": peer},
        device_id_type=MESH,
    )


def gi_send(n, f, gis, gi, gi_s, gi_r, own_s):
    for d in range(n - 1, 0, -1):
        @pl.when(f + d < n)
        def _():
            gi_copy(f + d, f, gis, gi, gi_s, gi_r).start()

        @pl.when(f - d >= 0)
        def _():
            gi_copy(f - d, f, gis, gi, gi_s, gi_r).start()

    pltpu.make_async_copy(gis.at[f], share_of(gi, f, gis.shape[2]), own_s).start()


def gi_wait(n, f, gis, gi, gi_s, gi_r, own_s):
    pltpu.make_async_copy(gis.at[f], share_of(gi, f, gis.shape[2]), own_s).wait()

    def run(step, carry):
        peer = lax.rem(f + step, n)
        gi_copy(peer, peer, gis, gi, gi_s, gi_r).wait()
        return carry

    lax.fori_loop(1, n, run, 0)


def kernel(
    n, ns, li, cot, w, mid, gi, gis, inc, lix, ids, wv,
    perm_s, perm_r, right_s, left_s, cot_r, li_s, li_r, gi_s, gi_r, id_s, id_r, own_s,
    above, below, pair,
):
    f = lax.axis_index("fsdp")
    s = lax.axis_index("section")
    behind = lax.rem(s + ns - 1, ns)
    ahead = lax.rem(s + 1, ns)
    at_once = lax.rem(s, 2) == AT_ONCE
    early_ahead = lax.rem(ahead, 4) != 0
    turns = (
        jnp.logical_not(at_once),
        at_once & early_ahead,
        at_once & jnp.logical_not(early_ahead) & (s < ns - 1),
        at_once & jnp.logical_not(early_ahead) & (s == ns - 1),
    )
    tokens, share = lix.shape[1], lix.shape[2]
    columns = inc.shape[2]

    def li_copy(target, rows=slice(None)):
        return pltpu.make_async_remote_copy(
            src_ref=share_of(li, target, share, rows),
            dst_ref=lix.at[f, rows],
            send_sem=li_s.at[target],
            recv_sem=li_r.at[f],
            device_id={"fsdp": target},
            device_id_type=MESH,
        )

    def cot_copy(block, target, sem):
        return pltpu.make_async_remote_copy(
            src_ref=inc.at[block],
            dst_ref=inc.at[block],
            send_sem=sem.at[block],
            recv_sem=cot_r.at[block],
            device_id={"fsdp": target},
            device_id_type=MESH,
        )

    def id_copy(target, owner):
        return pltpu.make_async_remote_copy(
            src_ref=ids.at[owner],
            dst_ref=ids.at[owner],
            send_sem=id_s.at[target],
            recv_sem=id_r.at[owner],
            device_id={"fsdp": target},
            device_id_type=MESH,
        )

    permute = pltpu.make_async_remote_copy(
        src_ref=cot,
        dst_ref=inc.at[f],
        send_sem=perm_s,
        recv_sem=perm_r,
        device_id={"section": behind},
        device_id_type=MESH,
    )
    weights = pltpu.make_async_copy(w, wv, own_s.at[0])
    own_li = pltpu.make_async_copy(share_of(li, f, share), lix.at[f], own_s.at[1])

    late, late_ahead = lax.rem(s, 4) == 0, lax.rem(ahead, 4) == 0
    barrier = pltpu.get_barrier_semaphore()
    tell(barrier, f + 1, f < n - 1)

    @pl.when(jnp.logical_not(late_ahead))
    def _():
        pl.semaphore_signal(barrier, inc=1, device_id={"section": ahead}, device_id_type=MESH)

    @pl.when(late)
    def _():
        pl.semaphore_signal(barrier, inc=1, device_id={"section": behind}, device_id_type=MESH)

    greetings = (f > 0).astype(jnp.int32) + 1 - late.astype(jnp.int32) + late_ahead.astype(jnp.int32)

    @pl.when(greetings > 0)
    def _():
        pl.semaphore_wait(barrier, greetings)

    @pl.when(late_ahead)
    def _():
        pl.semaphore_signal(pair, inc=1, device_id={"section": ahead}, device_id_type=MESH)

    pieces = PIECES
    rows = tokens // pieces

    half = n // 2
    total = half * pieces

    def head_rows(turn):
        return min(HEAD[turn], pieces) * rows

    def by_turn(action):
        for turn, condition in enumerate(turns):
            pl.when(condition)(functools.partial(action, turn))

    def crossing(index, turn):
        owner, piece = index // pieces, index % pieces
        window = pl.ds(piece * rows, rows)
        done = owner == half - 1 and piece * rows < head_rows(turn)

        @pl.when((f < half - 1) if done else (f < half))
        def _():
            li_copy(n - 1 - owner, window).start()

        @pl.when((f > half) if done else (f >= half))
        def _():
            li_copy(owner, window).start()

    def near(piece):
        if piece >= pieces:
            return
        window = pl.ds(piece * rows, rows)

        @pl.when((f > 0) & (f < half))
        def _():
            li_copy(0, window).start()

        @pl.when((f >= half) & (f < n - 1))
        def _():
            li_copy(n - 1, window).start()

    def inner():
        for distance in range(n - 1, 0, -1):
            @pl.when(f + distance < half)
            def _():
                li_copy(f + distance).start()

            @pl.when(f - distance >= half)
            def _():
                li_copy(f - distance).start()

    def forward(step):
        @pl.when((f - step >= 0) & (f < n - 1))
        def _():
            cot_copy(f - step, f + 1, right_s).start()

        @pl.when((f + step < n) & (f > 0))
        def _():
            cot_copy(f + step, f - 1, left_s).start()

    def arrived(step):
        @pl.when(f - step >= 0)
        def _():
            cot_copy(f - step, f, right_s).wait_recv()

        @pl.when(f + step < n)
        def _():
            cot_copy(f + step, f, left_s).wait_recv()

    tell(above.at[1], f - 1, f > 0)

    @pl.when(jnp.logical_not(late))
    def _():
        permute.start()

    @pl.when(f == half)
    def _():
        by_turn(lambda turn: li_copy(half - 1, pl.ds(0, head_rows(turn))).start())

    @pl.when(f < n - 1)
    def _():
        pl.semaphore_wait(above.at[1], 1)

    @pl.when(f == half - 1)
    def _():
        by_turn(lambda turn: li_copy(half, pl.ds(0, head_rows(turn))).start())

    if n > 2:
        tell(above.at[2], f - 1, (f > 0) & (f + 1 < n))
        tell(below.at[2], f + 1, (f < n - 1) & (f - 1 >= 0))
    near(0)
    weights.start()
    own_li.start()
    ids[f] = jnp.full(ids.shape[1:], mid[0, 0], jnp.int32)

    def late_permute():
        pl.semaphore_wait(pair, 1)
        permute.start()

    pl.when(late & (f == 0))(late_permute)
    for d in range(2, n):
        @pl.when(f + d < n)
        def _():
            pl.semaphore_wait(above.at[d], 1)

        @pl.when(f - d >= 0)
        def _():
            pl.semaphore_wait(below.at[d], 1)

        if d + 1 < n:
            tell(above.at[d + 1], f - 1, (f > 0) & (f + d < n))
            tell(below.at[d + 1], f + 1, (f < n - 1) & (f - d >= 0))

    pl.when(late & (f > 0))(late_permute)
    permute.wait_recv()
    forward(0)
    near(1)
    for step in range(1, n):
        target = lax.rem(f + step, n)
        id_copy(target, f).start()
    def quota(step, turn):
        return min(total, step * (BETWEEN[turn]))

    def crossings(step, turn):
        for index in range(quota(step - 1, turn), quota(step, turn)):
            crossing(index, turn)

    for step in range(1, n - 1):
        by_turn(functools.partial(crossings, step))
        arrived(step)
        forward(step)
        near(step + 1)
    for piece in range(n, pieces):
        near(piece)

    def remaining(turn):
        begin = quota(n - 2, turn)
        middle = min(max(begin, INNER), total)
        for index in range(begin, middle):
            crossing(index, turn)
        inner()
        for index in range(middle, total):
            crossing(index, turn)

    by_turn(remaining)
    for distance in range(n - 1, 0, -1):
        @pl.when((f >= half) & (f + distance < n - 1))
        def _():
            li_copy(f + distance).start()

        @pl.when((f < half) & (f - distance > 0))
        def _():
            li_copy(f - distance).start()

    weights.wait()

    def input_block(block):
        gis[block] = lax.dot_general(
            inc[block], wv[...], (((1,), (1,)), ((), ())), preferred_element_type=jnp.float32
        ).astype(gis.dtype)

    arrived(n - 1)

    def input_blocks(block, carry):
        input_block(block)
        return carry

    lax.fori_loop(0, n, input_blocks, 0)

    @pl.when(at_once)
    def _():
        gi_send(n, f, gis, gi, gi_s, gi_r, own_s.at[2])

    own_li.wait()

    def others(action):
        def run(step, carry):
            action(lax.rem(f + step, n))
            return carry

        lax.fori_loop(1, n, run, 0)

    def li_wait(peer):
        pltpu.make_async_remote_copy(
            src_ref=share_of(li, peer, share),
            dst_ref=lix.at[peer],
            send_sem=li_s.at[peer],
            recv_sem=li_r.at[peer],
            device_id={"fsdp": peer},
            device_id_type=MESH,
        ).wait()
        id_copy(peer, peer).wait()

    others(li_wait)

    permute.wait_send()
    for step in range(n - 1):
        @pl.when((f - step >= 0) & (f < n - 1))
        def _():
            cot_copy(f - step, f + 1, right_s).wait_send()

        @pl.when((f + step < n) & (f > 0))
        def _():
            cot_copy(f + step, f - 1, left_s).wait_send()

    @pl.when(at_once)
    def _():
        gi_wait(n, f, gis, gi, gi_s, gi_r, own_s.at[2])


def weight_kernel(n, inc, lix, ids, gs_out, gq_out, token, gs, gq, sems):
    tokens, share = lix.shape[1:]
    columns = inc.shape[2]
    inverse = 1.0 / tokens
    exact = tokens & (tokens - 1) == 0
    tile = min(TILE, share)
    outs = ((gs, gs_out), (gq, gq_out))

    def out_copy(index, which):
        window = pl.ds(pl.multiple_of(index * tile, tile), tile)
        source, target = outs[which]
        return pltpu.make_async_copy(source.at[window], target.at[window], sems.at[which, index])

    def weight_rows(index, carry):
        start = pl.multiple_of(index * tile, tile)
        total, micro = None, [None] * MICRO
        for block in range(n):
            product = lax.dot_general(
                lix[block, :, pl.ds(start, tile)],
                inc[block],
                (((0,), (0,)), ((), ())),
                preferred_element_type=jnp.float32,
            )
            if not exact:
                product = product * inverse
            product = product.astype(jnp.bfloat16).astype(jnp.float32)
            total = product if total is None else total + product
            for m in range(1, MICRO):
                part = product * (ids[block][:1, :1] == m).astype(jnp.float32)
                micro[m] = part if micro[m] is None else micro[m] + part
        micro[0] = total
        for m in range(1, MICRO):
            micro[0] = micro[0] - micro[m]
        square = micro[0] * micro[0]
        for m in range(1, MICRO):
            square = square + micro[m] * micro[m]
        if exact:
            total, square = total * inverse, square * (inverse * inverse)
        gs[pl.ds(start, tile), :] = total
        gq[pl.ds(start, tile), :] = square
        for which in range(2):
            out_copy(index, which).start()
        return carry

    lax.fori_loop(0, share // tile, weight_rows, 0)
    token[...] = jnp.zeros_like(token)

    def finish(index, carry):
        for which in range(2):
            out_copy(index, which).wait()
        return carry

    lax.fori_loop(0, share // tile, finish, 0)


def late_kernel(n, gis, token, gi, gi_s, gi_r, own_s, above, below):
    f = lax.axis_index("fsdp")
    s = lax.axis_index("section")
    half = n // 2

    tokens = gis.shape[1]
    cut = tokens // 2

    def send(peer, cond, rows=slice(None)):
        @pl.when(cond)
        def _():
            gi_copy(peer, f, gis, gi, gi_s, gi_r, rows).start()

    @pl.when(lax.rem(s, 2) != AT_ONCE)
    def _():
        barrier = pltpu.get_barrier_semaphore()
        tell(barrier, f + 1, f < n - 1)

        @pl.when(f > 0)
        def _():
            pl.semaphore_wait(barrier, 1)

        tell(above.at[1], f - 1, f > 0)
        send(half - 1, f == half, pl.ds(0, cut))
        send(f - 1, (f > 0) & (f < half))

        @pl.when(f < n - 1)
        def _():
            pl.semaphore_wait(above.at[1], 1)

        send(half, f == half - 1, pl.ds(0, cut))
        if n > 2:
            tell(above.at[2], f - 1, (f > 0) & (f + 1 < n))
            tell(below.at[2], f + 1, (f < n - 1) & (f - 1 >= 0))
        send(f + 1, (f >= half) & (f < n - 1))
        for d in range(2, n):
            @pl.when(f + d < n)
            def _():
                pl.semaphore_wait(above.at[d], 1)

            @pl.when(f - d >= 0)
            def _():
                pl.semaphore_wait(below.at[d], 1)

            if d + 1 < n:
                tell(above.at[d + 1], f - 1, (f > 0) & (f + d < n))
                tell(below.at[d + 1], f + 1, (f < n - 1) & (f - d >= 0))
        for d in range(n - 1, 1, -1):
            send(f + d, (f + d < n) & ((f >= half) | (f + d > half)))
            send(f - d, (f - d >= 0) & ((f < half) | (f - d < half - 1)))
        for d in range(n - 1, 0, -1):
            send(f + d, f + d < half)
            send(f - d, f - d >= half)
        send(half - 1, f == half, pl.ds(cut, tokens - cut))
        send(half, f == half - 1, pl.ds(cut, tokens - cut))
        send(half, f < half - 1)
        send(half - 1, f > half)
        pltpu.make_async_copy(gis.at[f], share_of(gi, f, gis.shape[2]), own_s).start()
        gi_wait(n, f, gis, gi, gi_s, gi_r, own_s)


def settle_kernel(early, late, out, sem):
    s = lax.axis_index("section")
    at_once = lax.rem(s, 2) == AT_ONCE

    @pl.when(at_once)
    def _():
        copy = pltpu.make_async_copy(early, out, sem)
        copy.start()
        copy.wait()

    @pl.when(jnp.logical_not(at_once))
    def _():
        copy = pltpu.make_async_copy(late, out, sem)
        copy.start()
        copy.wait()


def body(layer_input, next_cot, w_value, micro_ids):
    n = lax.axis_size("fsdp")
    ns = lax.axis_size("section")
    tokens, width = layer_input.shape[1:]
    share, columns = w_value.shape[1:]
    hbm, vmem = pl.BlockSpec(memory_space=pltpu.HBM), pl.BlockSpec(memory_space=pltpu.VMEM)
    anywhere = pl.BlockSpec(memory_space=pl.ANY)
    dma, regular = pltpu.SemaphoreType.DMA, pltpu.SemaphoreType.REGULAR
    shape = jax.ShapeDtypeStruct
    stay = functools.partial(pltpu.with_memory_space_constraint, memory_space=pltpu.HBM)
    near = functools.partial(pltpu.with_memory_space_constraint, memory_space=pltpu.VMEM)
    early, gis, inc, lix, ids = pl.pallas_call(
        functools.partial(kernel, n, ns),
        out_shape=(
            shape((tokens, width), jnp.bfloat16),
            shape((n, tokens, share), jnp.bfloat16),
            shape((n, tokens, columns), jnp.bfloat16),
            shape((n, tokens, share), jnp.bfloat16),
            shape((n, 8, 128), jnp.int32),
        ),
        in_specs=[hbm, hbm, hbm, pl.BlockSpec(memory_space=pltpu.SMEM)],
        out_specs=(anywhere, vmem, vmem, vmem, vmem),
        scratch_shapes=[
            pltpu.VMEM((share, columns), jnp.bfloat16),
            dma, dma, dma((n,)), dma((n,)), dma((n,)), dma((n,)), dma((n,)),
            dma((n,)), dma((n,)), dma((n,)), dma((n,)), dma((3,)),
            regular((n,)), regular((n,)), regular,
        ],
        compiler_params=pltpu.CompilerParams(
            collective_id=0, has_side_effects=True, vmem_limit_bytes=40 * 2**20
        ),
    )(stay(layer_input[0]), stay(next_cot[0]), stay(w_value[0]), micro_ids)
    wide = shape((share, columns), jnp.float32)
    grad_sum, grad_square, token = pl.pallas_call(
        functools.partial(weight_kernel, n),
        out_shape=(wide, wide, shape((8, 128), jnp.float32)),
        in_specs=[vmem, vmem, vmem],
        out_specs=(hbm, hbm, vmem),
        scratch_shapes=[
            pltpu.VMEM((share, columns), jnp.float32),
            pltpu.VMEM((share, columns), jnp.float32),
            dma((2, share // min(TILE, share))),
        ],
        compiler_params=pltpu.CompilerParams(vmem_limit_bytes=16 * 2**20),
    )(inc, lix, ids)
    late = pl.pallas_call(
        functools.partial(late_kernel, n),
        out_shape=shape((tokens, width), jnp.bfloat16),
        in_specs=[vmem, anywhere],
        out_specs=anywhere,
        scratch_shapes=[dma((n,)), dma((n,)), dma, regular((n,)), regular((n,))],
        compiler_params=pltpu.CompilerParams(
            collective_id=1, has_side_effects=True, vmem_limit_bytes=40 * 2**20
        ),
    )(gis, token)
    grad_input = pl.pallas_call(
        settle_kernel,
        out_shape=shape((tokens, width), jnp.bfloat16),
        in_specs=[anywhere, anywhere],
        out_specs=hbm,
        scratch_shapes=[dma],
        compiler_params=pltpu.CompilerParams(vmem_limit_bytes=4 * 2**20),
    )(near(early), near(late))
    return (grad_input[None], grad_sum[None], grad_square[None])


def solution(mesh):
    spec = P("section", "fsdp", None)
    return jax.shard_map(
        body,
        mesh=mesh,
        in_specs=(spec, spec, spec, P("section", "fsdp")),
        out_specs=(spec, spec, spec),
        check_vma=False,
    )
```

```python
import functools

import jax
import jax.numpy as jnp
from jax import lax
from jax.experimental import pallas as pl
from jax.experimental.pallas import tpu as pltpu
from jax.sharding import PartitionSpec as P

MICRO = 2
MESH = pl.DeviceIdType.MESH
PIECES = 4
HEAD = 3
BETWEEN = (1, 2)
TILE = 256
AT_ONCE = 0
INNER = 4


def tell(sem, target, cond):
    @pl.when(cond)
    def _():
        pl.semaphore_signal(sem, inc=1, device_id={"fsdp": target}, device_id_type=MESH)


def share_of(ref, part, share, rows=slice(None)):
    return ref.at[rows, pl.ds(pl.multiple_of(part * share, share), share)]


def gi_copy(peer, owner, gis, gi, gi_s, gi_r, rows=slice(None)):
    return pltpu.make_async_remote_copy(
        src_ref=gis.at[peer, rows],
        dst_ref=share_of(gi, owner, gis.shape[2], rows),
        send_sem=gi_s.at[peer],
        recv_sem=gi_r.at[owner],
        device_id={"fsdp": peer},
        device_id_type=MESH,
    )


def gi_send(n, f, gis, gi, gi_s, gi_r, own_s):
    for d in range(n - 1, 0, -1):
        @pl.when(f + d < n)
        def _():
            gi_copy(f + d, f, gis, gi, gi_s, gi_r).start()

        @pl.when(f - d >= 0)
        def _():
            gi_copy(f - d, f, gis, gi, gi_s, gi_r).start()

    pltpu.make_async_copy(gis.at[f], share_of(gi, f, gis.shape[2]), own_s).start()


def gi_wait(n, f, gis, gi, gi_s, gi_r, own_s):
    pltpu.make_async_copy(gis.at[f], share_of(gi, f, gis.shape[2]), own_s).wait()

    def run(step, carry):
        peer = lax.rem(f + step, n)
        gi_copy(peer, peer, gis, gi, gi_s, gi_r).wait()
        return carry

    lax.fori_loop(1, n, run, 0)


def kernel(
    n, ns, li, cot, w, mid, gi, gis, inc, lix, ids, wv,
    perm_s, perm_r, right_s, left_s, cot_r, li_s, li_r, gi_s, gi_r, id_s, id_r, own_s,
    above, below, pair,
):
    f = lax.axis_index("fsdp")
    s = lax.axis_index("section")
    behind = lax.rem(s + ns - 1, ns)
    ahead = lax.rem(s + 1, ns)
    at_once = lax.rem(s, 2) == AT_ONCE
    tokens, share = lix.shape[1], lix.shape[2]
    columns = inc.shape[2]

    def li_copy(target, rows=slice(None)):
        return pltpu.make_async_remote_copy(
            src_ref=share_of(li, target, share, rows),
            dst_ref=lix.at[f, rows],
            send_sem=li_s.at[target],
            recv_sem=li_r.at[f],
            device_id={"fsdp": target},
            device_id_type=MESH,
        )

    def cot_copy(block, target, sem):
        return pltpu.make_async_remote_copy(
            src_ref=inc.at[block],
            dst_ref=inc.at[block],
            send_sem=sem.at[block],
            recv_sem=cot_r.at[block],
            device_id={"fsdp": target},
            device_id_type=MESH,
        )

    def id_copy(target, owner):
        return pltpu.make_async_remote_copy(
            src_ref=ids.at[owner],
            dst_ref=ids.at[owner],
            send_sem=id_s.at[target],
            recv_sem=id_r.at[owner],
            device_id={"fsdp": target},
            device_id_type=MESH,
        )

    permute = pltpu.make_async_remote_copy(
        src_ref=cot,
        dst_ref=inc.at[f],
        send_sem=perm_s,
        recv_sem=perm_r,
        device_id={"section": behind},
        device_id_type=MESH,
    )
    weights = pltpu.make_async_copy(w, wv, own_s.at[0])
    own_li = pltpu.make_async_copy(share_of(li, f, share), lix.at[f], own_s.at[1])

    late, late_ahead = s == 0, ahead == 0
    barrier = pltpu.get_barrier_semaphore()
    tell(barrier, f + 1, f < n - 1)

    @pl.when(jnp.logical_not(late_ahead))
    def _():
        pl.semaphore_signal(barrier, inc=1, device_id={"section": ahead}, device_id_type=MESH)

    @pl.when(late)
    def _():
        pl.semaphore_signal(barrier, inc=1, device_id={"section": behind}, device_id_type=MESH)

    greetings = (f > 0).astype(jnp.int32) + 1 - late.astype(jnp.int32) + late_ahead.astype(jnp.int32)

    @pl.when(greetings > 0)
    def _():
        pl.semaphore_wait(barrier, greetings)

    @pl.when(late_ahead)
    def _():
        pl.semaphore_signal(pair, inc=1, device_id={"section": ahead}, device_id_type=MESH)

    pieces = PIECES
    rows = tokens // pieces

    half = n // 2
    total = half * pieces

    head = min(HEAD, pieces)

    def crossing(index):
        owner, piece = index // pieces, index % pieces
        window = pl.ds(piece * rows, rows)
        done = owner == half - 1 and piece < head

        @pl.when((f < half - 1) if done else (f < half))
        def _():
            li_copy(n - 1 - owner, window).start()

        @pl.when((f > half) if done else (f >= half))
        def _():
            li_copy(owner, window).start()

    def near(piece):
        if piece >= pieces:
            return
        window = pl.ds(piece * rows, rows)

        @pl.when((f > 0) & (f < half))
        def _():
            li_copy(0, window).start()

        @pl.when((f >= half) & (f < n - 1))
        def _():
            li_copy(n - 1, window).start()

    def inner():
        for distance in range(n - 1, 0, -1):
            @pl.when(f + distance < half)
            def _():
                li_copy(f + distance).start()

            @pl.when(f - distance >= half)
            def _():
                li_copy(f - distance).start()

    def forward(step):
        @pl.when((f - step >= 0) & (f < n - 1))
        def _():
            cot_copy(f - step, f + 1, right_s).start()

        @pl.when((f + step < n) & (f > 0))
        def _():
            cot_copy(f + step, f - 1, left_s).start()

    def arrived(step):
        @pl.when(f - step >= 0)
        def _():
            cot_copy(f - step, f, right_s).wait_recv()

        @pl.when(f + step < n)
        def _():
            cot_copy(f + step, f, left_s).wait_recv()

    tell(above.at[1], f - 1, f > 0)

    @pl.when(jnp.logical_not(late))
    def _():
        permute.start()

    @pl.when(f == half)
    def _():
        li_copy(half - 1, pl.ds(0, head * rows)).start()

    @pl.when(f < n - 1)
    def _():
        pl.semaphore_wait(above.at[1], 1)

    @pl.when(f == half - 1)
    def _():
        li_copy(half, pl.ds(0, head * rows)).start()

    if n > 2:
        tell(above.at[2], f - 1, (f > 0) & (f + 1 < n))
        tell(below.at[2], f + 1, (f < n - 1) & (f - 1 >= 0))
    near(0)
    weights.start()
    own_li.start()
    ids[f] = jnp.full(ids.shape[1:], mid[0, 0], jnp.int32)

    def late_permute():
        pl.semaphore_wait(pair, 1)
        permute.start()

    pl.when(late & (f == 0))(late_permute)
    for d in range(2, n):
        @pl.when(f + d < n)
        def _():
            pl.semaphore_wait(above.at[d], 1)

        @pl.when(f - d >= 0)
        def _():
            pl.semaphore_wait(below.at[d], 1)

        if d + 1 < n:
            tell(above.at[d + 1], f - 1, (f > 0) & (f + d < n))
            tell(below.at[d + 1], f + 1, (f < n - 1) & (f - d >= 0))

    pl.when(late & (f > 0))(late_permute)
    permute.wait_recv()
    forward(0)
    near(1)
    for step in range(1, n):
        target = lax.rem(f + step, n)
        id_copy(target, f).start()
    def by_section(action):
        for which, condition in enumerate((s < ns - 1, s == ns - 1)):
            pl.when(condition)(functools.partial(action, which))

    def quota(step, which):
        return min(total, step * BETWEEN[which])

    def crossings(step, which):
        for index in range(quota(step - 1, which), quota(step, which)):
            crossing(index)

    for step in range(1, n - 1):
        by_section(functools.partial(crossings, step))
        arrived(step)
        forward(step)
        near(step + 1)
    for piece in range(n, pieces):
        near(piece)

    def remaining(which):
        begin = quota(n - 2, which)
        middle = min(max(begin, INNER), total)
        for index in range(begin, middle):
            crossing(index)
        inner()
        for index in range(middle, total):
            crossing(index)

    by_section(remaining)
    for distance in range(n - 1, 0, -1):
        @pl.when((f >= half) & (f + distance < n - 1))
        def _():
            li_copy(f + distance).start()

        @pl.when((f < half) & (f - distance > 0))
        def _():
            li_copy(f - distance).start()

    weights.wait()

    def input_block(block):
        gis[block] = lax.dot_general(
            inc[block], wv[...], (((1,), (1,)), ((), ())), preferred_element_type=jnp.float32
        ).astype(gis.dtype)

    arrived(n - 1)

    def input_blocks(block, carry):
        input_block(block)
        return carry

    lax.fori_loop(0, n, input_blocks, 0)

    @pl.when(at_once)
    def _():
        gi_send(n, f, gis, gi, gi_s, gi_r, own_s.at[2])

    own_li.wait()

    def others(action):
        def run(step, carry):
            action(lax.rem(f + step, n))
            return carry

        lax.fori_loop(1, n, run, 0)

    def li_wait(peer):
        pltpu.make_async_remote_copy(
            src_ref=share_of(li, peer, share),
            dst_ref=lix.at[peer],
            send_sem=li_s.at[peer],
            recv_sem=li_r.at[peer],
            device_id={"fsdp": peer},
            device_id_type=MESH,
        ).wait()
        id_copy(peer, peer).wait()

    others(li_wait)

    permute.wait_send()
    for step in range(n - 1):
        @pl.when((f - step >= 0) & (f < n - 1))
        def _():
            cot_copy(f - step, f + 1, right_s).wait_send()

        @pl.when((f + step < n) & (f > 0))
        def _():
            cot_copy(f + step, f - 1, left_s).wait_send()

    @pl.when(at_once)
    def _():
        gi_wait(n, f, gis, gi, gi_s, gi_r, own_s.at[2])


def weight_kernel(n, inc, lix, ids, gs_out, gq_out, token, gs, gq, sems):
    tokens, share = lix.shape[1:]
    columns = inc.shape[2]
    inverse = 1.0 / tokens
    exact = tokens & (tokens - 1) == 0
    tile = min(TILE, share)
    outs = ((gs, gs_out), (gq, gq_out))

    def out_copy(index, which):
        window = pl.ds(pl.multiple_of(index * tile, tile), tile)
        source, target = outs[which]
        return pltpu.make_async_copy(source.at[window], target.at[window], sems.at[which, index])

    def weight_rows(index, carry):
        start = pl.multiple_of(index * tile, tile)
        total, micro = None, [None] * MICRO
        for block in range(n):
            product = lax.dot_general(
                lix[block, :, pl.ds(start, tile)],
                inc[block],
                (((0,), (0,)), ((), ())),
                preferred_element_type=jnp.float32,
            )
            if not exact:
                product = product * inverse
            product = product.astype(jnp.bfloat16).astype(jnp.float32)
            total = product if total is None else total + product
            for m in range(1, MICRO):
                part = product * (ids[block][:1, :1] == m).astype(jnp.float32)
                micro[m] = part if micro[m] is None else micro[m] + part
        micro[0] = total
        for m in range(1, MICRO):
            micro[0] = micro[0] - micro[m]
        square = micro[0] * micro[0]
        for m in range(1, MICRO):
            square = square + micro[m] * micro[m]
        if exact:
            total, square = total * inverse, square * (inverse * inverse)
        gs[pl.ds(start, tile), :] = total
        gq[pl.ds(start, tile), :] = square
        for which in range(2):
            out_copy(index, which).start()
        return carry

    lax.fori_loop(0, share // tile, weight_rows, 0)
    token[...] = jnp.zeros_like(token)

    def finish(index, carry):
        for which in range(2):
            out_copy(index, which).wait()
        return carry

    lax.fori_loop(0, share // tile, finish, 0)


def late_kernel(n, gis, token, gi, gi_s, gi_r, own_s, above, below):
    f = lax.axis_index("fsdp")
    s = lax.axis_index("section")
    half = n // 2

    tokens = gis.shape[1]
    cut = tokens // 2

    def send(peer, cond, rows=slice(None)):
        @pl.when(cond)
        def _():
            gi_copy(peer, f, gis, gi, gi_s, gi_r, rows).start()

    @pl.when(lax.rem(s, 2) != AT_ONCE)
    def _():
        barrier = pltpu.get_barrier_semaphore()
        tell(barrier, f + 1, f < n - 1)

        @pl.when(f > 0)
        def _():
            pl.semaphore_wait(barrier, 1)

        tell(above.at[1], f - 1, f > 0)
        send(half - 1, f == half, pl.ds(0, cut))
        send(f - 1, (f > 0) & (f < half))
        send(f - 1, f > half, pl.ds(0, cut))

        @pl.when(f < n - 1)
        def _():
            pl.semaphore_wait(above.at[1], 1)

        send(half, f == half - 1, pl.ds(0, cut))
        if n > 2:
            tell(above.at[2], f - 1, (f > 0) & (f + 1 < n))
            tell(below.at[2], f + 1, (f < n - 1) & (f - 1 >= 0))
        send(f + 1, (f >= half) & (f < n - 1))
        send(f + 1, f + 1 < half, pl.ds(0, cut))
        for d in range(2, n):
            @pl.when(f + d < n)
            def _():
                pl.semaphore_wait(above.at[d], 1)

            @pl.when(f - d >= 0)
            def _():
                pl.semaphore_wait(below.at[d], 1)

            if d + 1 < n:
                tell(above.at[d + 1], f - 1, (f > 0) & (f + d < n))
                tell(below.at[d + 1], f + 1, (f < n - 1) & (f - d >= 0))
        for d in range(n - 1, 1, -1):
            send(f + d, (f + d < n) & ((f >= half) | (f + d != half)))
            send(f - d, (f - d >= 0) & ((f < half) | (f - d != half - 1)))
        send(f - 1, f > half, pl.ds(cut, tokens - cut))
        send(f + 1, f + 1 < half, pl.ds(cut, tokens - cut))
        send(half, f < half - 1)
        send(half - 1, f > half)
        send(half - 1, f == half, pl.ds(cut, tokens - cut))
        send(half, f == half - 1, pl.ds(cut, tokens - cut))
        pltpu.make_async_copy(gis.at[f], share_of(gi, f, gis.shape[2]), own_s).start()
        gi_wait(n, f, gis, gi, gi_s, gi_r, own_s)


def settle_kernel(early, late, out, sem):
    s = lax.axis_index("section")
    at_once = lax.rem(s, 2) == AT_ONCE

    @pl.when(at_once)
    def _():
        copy = pltpu.make_async_copy(early, out, sem)
        copy.start()
        copy.wait()

    @pl.when(jnp.logical_not(at_once))
    def _():
        copy = pltpu.make_async_copy(late, out, sem)
        copy.start()
        copy.wait()


def body(layer_input, next_cot, w_value, micro_ids):
    n = lax.axis_size("fsdp")
    ns = lax.axis_size("section")
    tokens, width = layer_input.shape[1:]
    share, columns = w_value.shape[1:]
    hbm, vmem = pl.BlockSpec(memory_space=pltpu.HBM), pl.BlockSpec(memory_space=pltpu.VMEM)
    anywhere = pl.BlockSpec(memory_space=pl.ANY)
    dma, regular = pltpu.SemaphoreType.DMA, pltpu.SemaphoreType.REGULAR
    shape = jax.ShapeDtypeStruct
    stay = functools.partial(pltpu.with_memory_space_constraint, memory_space=pltpu.HBM)
    near = functools.partial(pltpu.with_memory_space_constraint, memory_space=pltpu.VMEM)
    early, gis, inc, lix, ids = pl.pallas_call(
        functools.partial(kernel, n, ns),
        out_shape=(
            shape((tokens, width), jnp.bfloat16),
            shape((n, tokens, share), jnp.bfloat16),
            shape((n, tokens, columns), jnp.bfloat16),
            shape((n, tokens, share), jnp.bfloat16),
            shape((n, 8, 128), jnp.int32),
        ),
        in_specs=[hbm, hbm, hbm, pl.BlockSpec(memory_space=pltpu.SMEM)],
        out_specs=(anywhere, vmem, vmem, vmem, vmem),
        scratch_shapes=[
            pltpu.VMEM((share, columns), jnp.bfloat16),
            dma, dma, dma((n,)), dma((n,)), dma((n,)), dma((n,)), dma((n,)),
            dma((n,)), dma((n,)), dma((n,)), dma((n,)), dma((3,)),
            regular((n,)), regular((n,)), regular,
        ],
        compiler_params=pltpu.CompilerParams(
            collective_id=0, has_side_effects=True, vmem_limit_bytes=40 * 2**20
        ),
    )(stay(layer_input[0]), stay(next_cot[0]), stay(w_value[0]), micro_ids)
    wide = shape((share, columns), jnp.float32)
    grad_sum, grad_square, token = pl.pallas_call(
        functools.partial(weight_kernel, n),
        out_shape=(wide, wide, shape((8, 128), jnp.float32)),
        in_specs=[vmem, vmem, vmem],
        out_specs=(hbm, hbm, vmem),
        scratch_shapes=[
            pltpu.VMEM((share, columns), jnp.float32),
            pltpu.VMEM((share, columns), jnp.float32),
            dma((2, share // min(TILE, share))),
        ],
        compiler_params=pltpu.CompilerParams(vmem_limit_bytes=16 * 2**20),
    )(inc, lix, ids)
    late = pl.pallas_call(
        functools.partial(late_kernel, n),
        out_shape=shape((tokens, width), jnp.bfloat16),
        in_specs=[vmem, anywhere],
        out_specs=anywhere,
        scratch_shapes=[dma((n,)), dma((n,)), dma, regular((n,)), regular((n,))],
        compiler_params=pltpu.CompilerParams(
            collective_id=1, has_side_effects=True, vmem_limit_bytes=40 * 2**20
        ),
    )(gis, token)
    grad_input = pl.pallas_call(
        settle_kernel,
        out_shape=shape((tokens, width), jnp.bfloat16),
        in_specs=[anywhere, anywhere],
        out_specs=hbm,
        scratch_shapes=[dma],
        compiler_params=pltpu.CompilerParams(vmem_limit_bytes=4 * 2**20),
    )(near(early), near(late))
    return (grad_input[None], grad_sum[None], grad_square[None])


def solution(mesh):
    spec = P("section", "fsdp", None)
    return jax.shard_map(
        body,
        mesh=mesh,
        in_specs=(spec, spec, spec, P("section", "fsdp")),
        out_specs=(spec, spec, spec),
        check_vma=False,
    )
```

```python
import functools

import jax
import jax.numpy as jnp
from jax import lax
from jax.experimental import pallas as pl
from jax.experimental.pallas import tpu as pltpu
from jax.sharding import PartitionSpec as P

MICRO = 2
MESH = pl.DeviceIdType.MESH
PIECES = 4
HEAD = 3
BETWEEN = (1, 2)
TILE = 256
AT_ONCE = 0
INNER = 4


def tell(sem, target, cond):
    @pl.when(cond)
    def _():
        pl.semaphore_signal(sem, inc=1, device_id={"fsdp": target}, device_id_type=MESH)


def share_of(ref, part, share, rows=slice(None)):
    return ref.at[rows, pl.ds(pl.multiple_of(part * share, share), share)]


def gi_copy(peer, owner, gis, gi, gi_s, gi_r, rows=slice(None)):
    return pltpu.make_async_remote_copy(
        src_ref=gis.at[peer, rows],
        dst_ref=share_of(gi, owner, gis.shape[2], rows),
        send_sem=gi_s.at[peer],
        recv_sem=gi_r.at[owner],
        device_id={"fsdp": peer},
        device_id_type=MESH,
    )


def gi_send(n, f, gis, gi, gi_s, gi_r, own_s):
    for d in range(n - 1, 0, -1):
        @pl.when(f + d < n)
        def _():
            gi_copy(f + d, f, gis, gi, gi_s, gi_r).start()

        @pl.when(f - d >= 0)
        def _():
            gi_copy(f - d, f, gis, gi, gi_s, gi_r).start()

    pltpu.make_async_copy(gis.at[f], share_of(gi, f, gis.shape[2]), own_s).start()


def gi_wait(n, f, gis, gi, gi_s, gi_r, own_s):
    pltpu.make_async_copy(gis.at[f], share_of(gi, f, gis.shape[2]), own_s).wait()

    def run(step, carry):
        peer = lax.rem(f + step, n)
        gi_copy(peer, peer, gis, gi, gi_s, gi_r).wait()
        return carry

    lax.fori_loop(1, n, run, 0)


def kernel(
    n, ns, li, cot, w, mid, gi, gis, inc, lix, ids, wv,
    perm_s, perm_r, right_s, left_s, cot_r, li_s, li_r, gi_s, gi_r, id_s, id_r, own_s,
    above, below, pair,
):
    f = lax.axis_index("fsdp")
    s = lax.axis_index("section")
    behind = lax.rem(s + ns - 1, ns)
    ahead = lax.rem(s + 1, ns)
    at_once = lax.rem(s, 2) == AT_ONCE
    tokens, share = lix.shape[1], lix.shape[2]
    columns = inc.shape[2]

    def li_copy(target, rows=slice(None)):
        return pltpu.make_async_remote_copy(
            src_ref=share_of(li, target, share, rows),
            dst_ref=lix.at[f, rows],
            send_sem=li_s.at[target],
            recv_sem=li_r.at[f],
            device_id={"fsdp": target},
            device_id_type=MESH,
        )

    def cot_copy(block, target, sem):
        return pltpu.make_async_remote_copy(
            src_ref=inc.at[block],
            dst_ref=inc.at[block],
            send_sem=sem.at[block],
            recv_sem=cot_r.at[block],
            device_id={"fsdp": target},
            device_id_type=MESH,
        )

    def id_copy(target, owner):
        return pltpu.make_async_remote_copy(
            src_ref=ids.at[owner],
            dst_ref=ids.at[owner],
            send_sem=id_s.at[target],
            recv_sem=id_r.at[owner],
            device_id={"fsdp": target},
            device_id_type=MESH,
        )

    permute = pltpu.make_async_remote_copy(
        src_ref=cot,
        dst_ref=inc.at[f],
        send_sem=perm_s,
        recv_sem=perm_r,
        device_id={"section": behind},
        device_id_type=MESH,
    )
    weights = pltpu.make_async_copy(w, wv, own_s.at[0])
    own_li = pltpu.make_async_copy(share_of(li, f, share), lix.at[f], own_s.at[1])

    late, late_ahead = s == 0, ahead == 0
    barrier = pltpu.get_barrier_semaphore()
    tell(barrier, f + 1, f < n - 1)

    @pl.when(jnp.logical_not(late_ahead))
    def _():
        pl.semaphore_signal(barrier, inc=1, device_id={"section": ahead}, device_id_type=MESH)

    @pl.when(late)
    def _():
        pl.semaphore_signal(barrier, inc=1, device_id={"section": behind}, device_id_type=MESH)

    greetings = (f > 0).astype(jnp.int32) + 1 - late.astype(jnp.int32) + late_ahead.astype(jnp.int32)

    @pl.when(greetings > 0)
    def _():
        pl.semaphore_wait(barrier, greetings)

    @pl.when(late_ahead)
    def _():
        pl.semaphore_signal(pair, inc=1, device_id={"section": ahead}, device_id_type=MESH)

    pieces = PIECES
    rows = tokens // pieces

    half = n // 2
    total = half * pieces

    head = min(HEAD, pieces)

    def crossing(index):
        owner, piece = index // pieces, index % pieces
        window = pl.ds(piece * rows, rows)
        done = owner == half - 1 and piece < head

        @pl.when((f < half - 1) if done else (f < half))
        def _():
            li_copy(n - 1 - owner, window).start()

        @pl.when((f > half) if done else (f >= half))
        def _():
            li_copy(owner, window).start()

    def near(piece):
        if piece >= pieces:
            return
        window = pl.ds(piece * rows, rows)

        @pl.when((f > 0) & (f < half))
        def _():
            li_copy(0, window).start()

        @pl.when((f >= half) & (f < n - 1))
        def _():
            li_copy(n - 1, window).start()

    def inner():
        for distance in range(n - 1, 0, -1):
            @pl.when(f + distance < half)
            def _():
                li_copy(f + distance).start()

            @pl.when(f - distance >= half)
            def _():
                li_copy(f - distance).start()

    def forward(step):
        @pl.when((f - step >= 0) & (f < n - 1))
        def _():
            cot_copy(f - step, f + 1, right_s).start()

        @pl.when((f + step < n) & (f > 0))
        def _():
            cot_copy(f + step, f - 1, left_s).start()

    def arrived(step):
        @pl.when(f - step >= 0)
        def _():
            cot_copy(f - step, f, right_s).wait_recv()

        @pl.when(f + step < n)
        def _():
            cot_copy(f + step, f, left_s).wait_recv()

    tell(above.at[1], f - 1, f > 0)

    @pl.when(jnp.logical_not(late))
    def _():
        permute.start()

    @pl.when(f == half)
    def _():
        li_copy(half - 1, pl.ds(0, head * rows)).start()

    @pl.when(f < n - 1)
    def _():
        pl.semaphore_wait(above.at[1], 1)

    @pl.when(f == half - 1)
    def _():
        li_copy(half, pl.ds(0, head * rows)).start()

    if n > 2:
        tell(above.at[2], f - 1, (f > 0) & (f + 1 < n))
        tell(below.at[2], f + 1, (f < n - 1) & (f - 1 >= 0))
    near(0)
    weights.start()
    own_li.start()
    ids[f] = jnp.full(ids.shape[1:], mid[0, 0], jnp.int32)

    def late_permute():
        pl.semaphore_wait(pair, 1)
        permute.start()

    pl.when(late & (f == 0))(late_permute)
    for d in range(2, n):
        @pl.when(f + d < n)
        def _():
            pl.semaphore_wait(above.at[d], 1)

        @pl.when(f - d >= 0)
        def _():
            pl.semaphore_wait(below.at[d], 1)

        if d + 1 < n:
            tell(above.at[d + 1], f - 1, (f > 0) & (f + d < n))
            tell(below.at[d + 1], f + 1, (f < n - 1) & (f - d >= 0))

    pl.when(late & (f > 0))(late_permute)
    permute.wait_recv()
    forward(0)
    near(1)
    for step in range(1, n):
        target = lax.rem(f + step, n)
        id_copy(target, f).start()
    def by_section(action):
        for which, condition in enumerate((s < ns - 1, s == ns - 1)):
            pl.when(condition)(functools.partial(action, which))

    def quota(step, which):
        return min(total, step * BETWEEN[which])

    def crossings(step, which):
        for index in range(quota(step - 1, which), quota(step, which)):
            crossing(index)

    for step in range(1, n - 1):
        by_section(functools.partial(crossings, step))
        arrived(step)
        forward(step)
        near(step + 1)
    for piece in range(n, pieces):
        near(piece)

    def remaining(which):
        begin = quota(n - 2, which)
        middle = min(max(begin, INNER), total)
        for index in range(begin, middle):
            crossing(index)
        inner()
        for index in range(middle, total):
            crossing(index)

    by_section(remaining)
    for distance in range(n - 1, 0, -1):
        @pl.when((f >= half) & (f + distance < n - 1))
        def _():
            li_copy(f + distance).start()

        @pl.when((f < half) & (f - distance > 0))
        def _():
            li_copy(f - distance).start()

    weights.wait()

    def input_block(block):
        gis[block] = lax.dot_general(
            inc[block], wv[...], (((1,), (1,)), ((), ())), preferred_element_type=jnp.float32
        ).astype(gis.dtype)

    arrived(n - 1)

    def input_blocks(block, carry):
        input_block(block)
        return carry

    lax.fori_loop(0, n, input_blocks, 0)

    @pl.when(at_once)
    def _():
        gi_send(n, f, gis, gi, gi_s, gi_r, own_s.at[2])

    own_li.wait()

    def others(action):
        def run(step, carry):
            action(lax.rem(f + step, n))
            return carry

        lax.fori_loop(1, n, run, 0)

    def li_wait(peer):
        pltpu.make_async_remote_copy(
            src_ref=share_of(li, peer, share),
            dst_ref=lix.at[peer],
            send_sem=li_s.at[peer],
            recv_sem=li_r.at[peer],
            device_id={"fsdp": peer},
            device_id_type=MESH,
        ).wait()
        id_copy(peer, peer).wait()

    others(li_wait)

    permute.wait_send()
    for step in range(n - 1):
        @pl.when((f - step >= 0) & (f < n - 1))
        def _():
            cot_copy(f - step, f + 1, right_s).wait_send()

        @pl.when((f + step < n) & (f > 0))
        def _():
            cot_copy(f + step, f - 1, left_s).wait_send()

    @pl.when(at_once)
    def _():
        gi_wait(n, f, gis, gi, gi_s, gi_r, own_s.at[2])


def weight_kernel(n, inc, lix, ids, gs_out, gq_out, token, gs, gq, sems):
    tokens, share = lix.shape[1:]
    columns = inc.shape[2]
    inverse = 1.0 / tokens
    exact = tokens & (tokens - 1) == 0
    tile = min(TILE, share)
    outs = ((gs, gs_out), (gq, gq_out))

    def out_copy(index, which):
        window = pl.ds(pl.multiple_of(index * tile, tile), tile)
        source, target = outs[which]
        return pltpu.make_async_copy(source.at[window], target.at[window], sems.at[which, index])

    def weight_rows(index, carry):
        start = pl.multiple_of(index * tile, tile)
        total, micro = None, [None] * MICRO
        for block in range(n):
            product = lax.dot_general(
                lix[block, :, pl.ds(start, tile)],
                inc[block],
                (((0,), (0,)), ((), ())),
                preferred_element_type=jnp.float32,
            )
            if not exact:
                product = product * inverse
            product = product.astype(jnp.bfloat16).astype(jnp.float32)
            total = product if total is None else total + product
            for m in range(1, MICRO):
                part = product * (ids[block][:1, :1] == m).astype(jnp.float32)
                micro[m] = part if micro[m] is None else micro[m] + part
        micro[0] = total
        for m in range(1, MICRO):
            micro[0] = micro[0] - micro[m]
        square = micro[0] * micro[0]
        for m in range(1, MICRO):
            square = square + micro[m] * micro[m]
        if exact:
            total, square = total * inverse, square * (inverse * inverse)
        gs[pl.ds(start, tile), :] = total
        gq[pl.ds(start, tile), :] = square
        for which in range(2):
            out_copy(index, which).start()
        return carry

    lax.fori_loop(0, share // tile, weight_rows, 0)
    token[...] = jnp.zeros_like(token)

    def finish(index, carry):
        for which in range(2):
            out_copy(index, which).wait()
        return carry

    lax.fori_loop(0, share // tile, finish, 0)


def late_kernel(n, gis, token, gi, gi_s, gi_r, own_s, above, below):
    f = lax.axis_index("fsdp")
    s = lax.axis_index("section")
    half = n // 2

    tokens = gis.shape[1]
    cut = tokens // 2

    def send(peer, cond, rows=slice(None)):
        @pl.when(cond)
        def _():
            gi_copy(peer, f, gis, gi, gi_s, gi_r, rows).start()

    @pl.when(lax.rem(s, 2) != AT_ONCE)
    def _():
        barrier = pltpu.get_barrier_semaphore()
        tell(barrier, f + 1, f < n - 1)

        @pl.when(f > 0)
        def _():
            pl.semaphore_wait(barrier, 1)

        tell(above.at[1], f - 1, f > 0)
        send(half - 1, f == half, pl.ds(0, cut))
        send(f - 1, (f > 0) & (f < half))
        send(f - 1, f > half, pl.ds(0, cut))

        @pl.when(f < n - 1)
        def _():
            pl.semaphore_wait(above.at[1], 1)

        send(half, f == half - 1, pl.ds(0, cut))
        if n > 2:
            tell(above.at[2], f - 1, (f > 0) & (f + 1 < n))
            tell(below.at[2], f + 1, (f < n - 1) & (f - 1 >= 0))
        send(f + 1, (f >= half) & (f < n - 1))
        send(f + 1, f + 1 < half, pl.ds(0, cut))
        for d in range(2, n):
            @pl.when(f + d < n)
            def _():
                pl.semaphore_wait(above.at[d], 1)

            @pl.when(f - d >= 0)
            def _():
                pl.semaphore_wait(below.at[d], 1)

            if d + 1 < n:
                tell(above.at[d + 1], f - 1, (f > 0) & (f + d < n))
                tell(below.at[d + 1], f + 1, (f < n - 1) & (f - d >= 0))
        for d in range(n - 1, 1, -1):
            send(f + d, (f + d < n) & ((f >= half) | (f + d != half)))
            send(f - d, (f - d >= 0) & ((f < half) | (f - d != half - 1)))
        send(f - 1, f > half, pl.ds(cut, tokens - cut))
        send(f + 1, f + 1 < half, pl.ds(cut, tokens - cut))
        send(half, f < half - 1)
        send(half - 1, f > half)
        send(half - 1, f == half, pl.ds(cut, tokens - cut))
        send(half, f == half - 1, pl.ds(cut, tokens - cut))
        pltpu.make_async_copy(gis.at[f], share_of(gi, f, gis.shape[2]), own_s).start()
        gi_wait(n, f, gis, gi, gi_s, gi_r, own_s)


def settle_kernel(early, late, out, sem):
    s = lax.axis_index("section")
    at_once = lax.rem(s, 2) == AT_ONCE
    parts = sem.shape[0]
    rows = out.shape[0] // parts

    def settle(source):
        copies = [
            pltpu.make_async_copy(source.at[pl.ds(p * rows, rows)], out.at[pl.ds(p * rows, rows)], sem.at[p])
            for p in range(parts)
        ]
        for copy in copies:
            copy.start()
        for copy in copies:
            copy.wait()

    pl.when(at_once)(functools.partial(settle, early))
    pl.when(jnp.logical_not(at_once))(functools.partial(settle, late))


def body(layer_input, next_cot, w_value, micro_ids):
    n = lax.axis_size("fsdp")
    ns = lax.axis_size("section")
    tokens, width = layer_input.shape[1:]
    share, columns = w_value.shape[1:]
    hbm, vmem = pl.BlockSpec(memory_space=pltpu.HBM), pl.BlockSpec(memory_space=pltpu.VMEM)
    anywhere = pl.BlockSpec(memory_space=pl.ANY)
    dma, regular = pltpu.SemaphoreType.DMA, pltpu.SemaphoreType.REGULAR
    shape = jax.ShapeDtypeStruct
    stay = functools.partial(pltpu.with_memory_space_constraint, memory_space=pltpu.HBM)
    near = functools.partial(pltpu.with_memory_space_constraint, memory_space=pltpu.VMEM)
    early, gis, inc, lix, ids = pl.pallas_call(
        functools.partial(kernel, n, ns),
        out_shape=(
            shape((tokens, width), jnp.bfloat16),
            shape((n, tokens, share), jnp.bfloat16),
            shape((n, tokens, columns), jnp.bfloat16),
            shape((n, tokens, share), jnp.bfloat16),
            shape((n, 8, 128), jnp.int32),
        ),
        in_specs=[hbm, hbm, hbm, pl.BlockSpec(memory_space=pltpu.SMEM)],
        out_specs=(anywhere, vmem, vmem, vmem, vmem),
        scratch_shapes=[
            pltpu.VMEM((share, columns), jnp.bfloat16),
            dma, dma, dma((n,)), dma((n,)), dma((n,)), dma((n,)), dma((n,)),
            dma((n,)), dma((n,)), dma((n,)), dma((n,)), dma((3,)),
            regular((n,)), regular((n,)), regular,
        ],
        compiler_params=pltpu.CompilerParams(
            collective_id=0, has_side_effects=True, vmem_limit_bytes=40 * 2**20
        ),
    )(stay(layer_input[0]), stay(next_cot[0]), stay(w_value[0]), micro_ids)
    wide = shape((share, columns), jnp.float32)
    grad_sum, grad_square, token = pl.pallas_call(
        functools.partial(weight_kernel, n),
        out_shape=(wide, wide, shape((8, 128), jnp.float32)),
        in_specs=[vmem, vmem, vmem],
        out_specs=(hbm, hbm, vmem),
        scratch_shapes=[
            pltpu.VMEM((share, columns), jnp.float32),
            pltpu.VMEM((share, columns), jnp.float32),
            dma((2, share // min(TILE, share))),
        ],
        compiler_params=pltpu.CompilerParams(vmem_limit_bytes=16 * 2**20),
    )(inc, lix, ids)
    late = pl.pallas_call(
        functools.partial(late_kernel, n),
        out_shape=shape((tokens, width), jnp.bfloat16),
        in_specs=[vmem, anywhere],
        out_specs=anywhere,
        scratch_shapes=[dma((n,)), dma((n,)), dma, regular((n,)), regular((n,))],
        compiler_params=pltpu.CompilerParams(
            collective_id=1, has_side_effects=True, vmem_limit_bytes=40 * 2**20
        ),
    )(gis, token)
    grad_input = pl.pallas_call(
        settle_kernel,
        out_shape=shape((tokens, width), jnp.bfloat16),
        in_specs=[anywhere, anywhere],
        out_specs=hbm,
        scratch_shapes=[dma((4,))],
        compiler_params=pltpu.CompilerParams(vmem_limit_bytes=4 * 2**20),
    )(near(early), near(late))
    return (grad_input[None], grad_sum[None], grad_square[None])


def solution(mesh):
    spec = P("section", "fsdp", None)
    return jax.shard_map(
        body,
        mesh=mesh,
        in_specs=(spec, spec, spec, P("section", "fsdp")),
        out_specs=(spec, spec, spec),
        check_vma=False,
    )
```

```python
import functools

import jax
import jax.numpy as jnp
from jax import lax
from jax.experimental import pallas as pl
from jax.experimental.pallas import tpu as pltpu
from jax.sharding import PartitionSpec as P

MICRO = 2
MESH = pl.DeviceIdType.MESH
PIECES = 4
HEAD = 3
BETWEEN = (1, 2)
TILE = 256
AT_ONCE = 0
INNER = 4


def tell(sem, target, cond):
    @pl.when(cond)
    def _():
        pl.semaphore_signal(sem, inc=1, device_id={"fsdp": target}, device_id_type=MESH)


def share_of(ref, part, share, rows=slice(None)):
    return ref.at[rows, pl.ds(pl.multiple_of(part * share, share), share)]


def gi_copy(peer, owner, gis, gi, gi_s, gi_r, rows=slice(None)):
    return pltpu.make_async_remote_copy(
        src_ref=gis.at[peer, rows],
        dst_ref=share_of(gi, owner, gis.shape[2], rows),
        send_sem=gi_s.at[peer],
        recv_sem=gi_r.at[owner],
        device_id={"fsdp": peer},
        device_id_type=MESH,
    )


def gi_send(n, f, gis, gi, gi_s, gi_r, own_s):
    for d in range(n - 1, 0, -1):
        @pl.when(f + d < n)
        def _():
            gi_copy(f + d, f, gis, gi, gi_s, gi_r).start()

        @pl.when(f - d >= 0)
        def _():
            gi_copy(f - d, f, gis, gi, gi_s, gi_r).start()

    pltpu.make_async_copy(gis.at[f], share_of(gi, f, gis.shape[2]), own_s).start()


def gi_wait(n, f, gis, gi, gi_s, gi_r, own_s):
    pltpu.make_async_copy(gis.at[f], share_of(gi, f, gis.shape[2]), own_s).wait()

    def run(step, carry):
        peer = lax.rem(f + step, n)
        gi_copy(peer, peer, gis, gi, gi_s, gi_r).wait()
        return carry

    lax.fori_loop(1, n, run, 0)


def kernel(
    n, ns, li, cot, w, mid, gi, gis, inc, lix, ids, wv,
    perm_s, perm_r, right_s, left_s, cot_r, li_s, li_r, gi_s, gi_r, id_s, id_r, own_s,
    above, below, pair, ready,
):
    f = lax.axis_index("fsdp")
    s = lax.axis_index("section")
    behind = lax.rem(s + ns - 1, ns)
    ahead = lax.rem(s + 1, ns)
    at_once = lax.rem(s, 2) == AT_ONCE
    tokens, share = lix.shape[1], lix.shape[2]
    columns = inc.shape[2]

    def li_copy(target, rows=slice(None)):
        return pltpu.make_async_remote_copy(
            src_ref=share_of(li, target, share, rows),
            dst_ref=lix.at[f, rows],
            send_sem=li_s.at[target],
            recv_sem=li_r.at[f],
            device_id={"fsdp": target},
            device_id_type=MESH,
        )

    def cot_copy(block, target, sem):
        return pltpu.make_async_remote_copy(
            src_ref=inc.at[block],
            dst_ref=inc.at[block],
            send_sem=sem.at[block],
            recv_sem=cot_r.at[block],
            device_id={"fsdp": target},
            device_id_type=MESH,
        )

    def id_copy(target, owner):
        return pltpu.make_async_remote_copy(
            src_ref=ids.at[owner],
            dst_ref=ids.at[owner],
            send_sem=id_s.at[target],
            recv_sem=id_r.at[owner],
            device_id={"fsdp": target},
            device_id_type=MESH,
        )

    permute = pltpu.make_async_remote_copy(
        src_ref=cot,
        dst_ref=inc.at[f],
        send_sem=perm_s,
        recv_sem=perm_r,
        device_id={"section": behind},
        device_id_type=MESH,
    )
    weights = pltpu.make_async_copy(w, wv, own_s.at[0])
    own_li = pltpu.make_async_copy(share_of(li, f, share), lix.at[f], own_s.at[1])

    pieces = PIECES
    rows = tokens // pieces
    half = n // 2
    total = half * pieces
    head = min(HEAD, pieces)
    opposite = 2 * half - 1 - f
    first_window = pl.ds(0, head * rows)
    staged = ((f == half - 1) | (f == half)) & (s < ns - 2)

    first_rows = pltpu.make_async_copy(share_of(li, opposite, share, first_window), ready, own_s.at[3])
    pl.when(staged)(first_rows.start)

    def send_first_rows():
        @pl.when(staged)
        def _():
            first_rows.wait()
            pltpu.make_async_remote_copy(
                src_ref=ready,
                dst_ref=lix.at[f, first_window],
                send_sem=li_s.at[opposite],
                recv_sem=li_r.at[f],
                device_id={"fsdp": opposite},
                device_id_type=MESH,
            ).start()

        @pl.when(jnp.logical_not(staged))
        def _():
            li_copy(opposite, first_window).start()

    late, late_ahead = s == 0, ahead == 0
    barrier = pltpu.get_barrier_semaphore()
    tell(barrier, f + 1, f < n - 1)

    @pl.when(jnp.logical_not(late_ahead))
    def _():
        pl.semaphore_signal(barrier, inc=1, device_id={"section": ahead}, device_id_type=MESH)

    @pl.when(late)
    def _():
        pl.semaphore_signal(barrier, inc=1, device_id={"section": behind}, device_id_type=MESH)

    greetings = (f > 0).astype(jnp.int32) + 1 - late.astype(jnp.int32) + late_ahead.astype(jnp.int32)

    @pl.when(greetings > 0)
    def _():
        pl.semaphore_wait(barrier, greetings)

    @pl.when(late_ahead)
    def _():
        pl.semaphore_signal(pair, inc=1, device_id={"section": ahead}, device_id_type=MESH)

    def crossing(index):
        owner, piece = index // pieces, index % pieces
        window = pl.ds(piece * rows, rows)
        done = owner == half - 1 and piece < head

        @pl.when((f < half - 1) if done else (f < half))
        def _():
            li_copy(n - 1 - owner, window).start()

        @pl.when((f > half) if done else (f >= half))
        def _():
            li_copy(owner, window).start()

    def near(piece):
        if piece >= pieces:
            return
        window = pl.ds(piece * rows, rows)

        @pl.when((f > 0) & (f < half))
        def _():
            li_copy(0, window).start()

        @pl.when((f >= half) & (f < n - 1))
        def _():
            li_copy(n - 1, window).start()

    def inner():
        for distance in range(n - 1, 0, -1):
            @pl.when(f + distance < half)
            def _():
                li_copy(f + distance).start()

            @pl.when(f - distance >= half)
            def _():
                li_copy(f - distance).start()

    def forward(step):
        @pl.when((f - step >= 0) & (f < n - 1))
        def _():
            cot_copy(f - step, f + 1, right_s).start()

        @pl.when((f + step < n) & (f > 0))
        def _():
            cot_copy(f + step, f - 1, left_s).start()

    def arrived(step):
        @pl.when(f - step >= 0)
        def _():
            cot_copy(f - step, f, right_s).wait_recv()

        @pl.when(f + step < n)
        def _():
            cot_copy(f + step, f, left_s).wait_recv()

    tell(above.at[1], f - 1, f > 0)

    @pl.when(jnp.logical_not(late))
    def _():
        permute.start()

    @pl.when(f == half)
    def _():
        send_first_rows()

    @pl.when(f < n - 1)
    def _():
        pl.semaphore_wait(above.at[1], 1)

    @pl.when(f == half - 1)
    def _():
        send_first_rows()

    if n > 2:
        tell(above.at[2], f - 1, (f > 0) & (f + 1 < n))
        tell(below.at[2], f + 1, (f < n - 1) & (f - 1 >= 0))
    near(0)
    weights.start()
    own_li.start()
    ids[f] = jnp.full(ids.shape[1:], mid[0, 0], jnp.int32)

    def late_permute():
        pl.semaphore_wait(pair, 1)
        permute.start()

    pl.when(late & (f == 0))(late_permute)
    for d in range(2, n):
        @pl.when(f + d < n)
        def _():
            pl.semaphore_wait(above.at[d], 1)

        @pl.when(f - d >= 0)
        def _():
            pl.semaphore_wait(below.at[d], 1)

        if d + 1 < n:
            tell(above.at[d + 1], f - 1, (f > 0) & (f + d < n))
            tell(below.at[d + 1], f + 1, (f < n - 1) & (f - d >= 0))

    pl.when(late & (f > 0))(late_permute)
    permute.wait_recv()
    forward(0)
    near(1)
    for step in range(1, n):
        target = lax.rem(f + step, n)
        id_copy(target, f).start()
    def by_section(action):
        for which, condition in enumerate((s < ns - 1, s == ns - 1)):
            pl.when(condition)(functools.partial(action, which))

    def quota(step, which):
        return min(total, step * BETWEEN[which])

    def crossings(step, which):
        for index in range(quota(step - 1, which), quota(step, which)):
            crossing(index)

    for step in range(1, n - 1):
        by_section(functools.partial(crossings, step))
        arrived(step)
        forward(step)
        near(step + 1)
    for piece in range(n, pieces):
        near(piece)

    def remaining(which):
        begin = quota(n - 2, which)
        middle = min(max(begin, INNER), total)
        for index in range(begin, middle):
            crossing(index)
        inner()
        for index in range(middle, total):
            crossing(index)

    by_section(remaining)
    for distance in range(n - 1, 0, -1):
        @pl.when((f >= half) & (f + distance < n - 1))
        def _():
            li_copy(f + distance).start()

        @pl.when((f < half) & (f - distance > 0))
        def _():
            li_copy(f - distance).start()

    weights.wait()

    def input_block(block):
        gis[block] = lax.dot_general(
            inc[block], wv[...], (((1,), (1,)), ((), ())), preferred_element_type=jnp.float32
        ).astype(gis.dtype)

    arrived(n - 1)

    def input_blocks(block, carry):
        input_block(block)
        return carry

    lax.fori_loop(0, n, input_blocks, 0)

    @pl.when(at_once)
    def _():
        gi_send(n, f, gis, gi, gi_s, gi_r, own_s.at[2])

    own_li.wait()

    def others(action):
        def run(step, carry):
            action(lax.rem(f + step, n))
            return carry

        lax.fori_loop(1, n, run, 0)

    def li_wait(peer):
        pltpu.make_async_remote_copy(
            src_ref=share_of(li, peer, share),
            dst_ref=lix.at[peer],
            send_sem=li_s.at[peer],
            recv_sem=li_r.at[peer],
            device_id={"fsdp": peer},
            device_id_type=MESH,
        ).wait()
        id_copy(peer, peer).wait()

    others(li_wait)

    permute.wait_send()
    for step in range(n - 1):
        @pl.when((f - step >= 0) & (f < n - 1))
        def _():
            cot_copy(f - step, f + 1, right_s).wait_send()

        @pl.when((f + step < n) & (f > 0))
        def _():
            cot_copy(f + step, f - 1, left_s).wait_send()

    @pl.when(at_once)
    def _():
        gi_wait(n, f, gis, gi, gi_s, gi_r, own_s.at[2])


def weight_kernel(n, inc, lix, ids, gs_out, gq_out, token, gs, gq, sems):
    tokens, share = lix.shape[1:]
    columns = inc.shape[2]
    inverse = 1.0 / tokens
    exact = tokens & (tokens - 1) == 0
    tile = min(TILE, share)
    outs = ((gs, gs_out), (gq, gq_out))

    def out_copy(index, which):
        window = pl.ds(pl.multiple_of(index * tile, tile), tile)
        source, target = outs[which]
        return pltpu.make_async_copy(source.at[window], target.at[window], sems.at[which, index])

    def weight_rows(index, carry):
        start = pl.multiple_of(index * tile, tile)
        total, micro = None, [None] * MICRO
        for block in range(n):
            product = lax.dot_general(
                lix[block, :, pl.ds(start, tile)],
                inc[block],
                (((0,), (0,)), ((), ())),
                preferred_element_type=jnp.float32,
            )
            if not exact:
                product = product * inverse
            product = product.astype(jnp.bfloat16).astype(jnp.float32)
            total = product if total is None else total + product
            for m in range(1, MICRO):
                part = product * (ids[block][:1, :1] == m).astype(jnp.float32)
                micro[m] = part if micro[m] is None else micro[m] + part
        micro[0] = total
        for m in range(1, MICRO):
            micro[0] = micro[0] - micro[m]
        square = micro[0] * micro[0]
        for m in range(1, MICRO):
            square = square + micro[m] * micro[m]
        if exact:
            total, square = total * inverse, square * (inverse * inverse)
        gs[pl.ds(start, tile), :] = total
        gq[pl.ds(start, tile), :] = square
        for which in range(2):
            out_copy(index, which).start()
        return carry

    lax.fori_loop(0, share // tile, weight_rows, 0)
    token[...] = jnp.zeros_like(token)

    def finish(index, carry):
        for which in range(2):
            out_copy(index, which).wait()
        return carry

    lax.fori_loop(0, share // tile, finish, 0)


def late_kernel(n, gis, token, gi, gi_s, gi_r, own_s, above, below):
    f = lax.axis_index("fsdp")
    s = lax.axis_index("section")
    half = n // 2

    tokens = gis.shape[1]
    cut = tokens // 2

    def send(peer, cond, rows=slice(None)):
        @pl.when(cond)
        def _():
            gi_copy(peer, f, gis, gi, gi_s, gi_r, rows).start()

    @pl.when(lax.rem(s, 2) != AT_ONCE)
    def _():
        barrier = pltpu.get_barrier_semaphore()
        tell(barrier, f + 1, f < n - 1)

        @pl.when(f > 0)
        def _():
            pl.semaphore_wait(barrier, 1)

        tell(above.at[1], f - 1, f > 0)
        send(half - 1, f == half, pl.ds(0, cut))
        send(f - 1, (f > 0) & (f < half))
        send(f - 1, f > half, pl.ds(0, cut))

        @pl.when(f < n - 1)
        def _():
            pl.semaphore_wait(above.at[1], 1)

        send(half, f == half - 1, pl.ds(0, cut))
        if n > 2:
            tell(above.at[2], f - 1, (f > 0) & (f + 1 < n))
            tell(below.at[2], f + 1, (f < n - 1) & (f - 1 >= 0))
        send(f + 1, (f >= half) & (f < n - 1))
        send(f + 1, f + 1 < half, pl.ds(0, cut))
        for d in range(2, n):
            @pl.when(f + d < n)
            def _():
                pl.semaphore_wait(above.at[d], 1)

            @pl.when(f - d >= 0)
            def _():
                pl.semaphore_wait(below.at[d], 1)

            if d + 1 < n:
                tell(above.at[d + 1], f - 1, (f > 0) & (f + d < n))
                tell(below.at[d + 1], f + 1, (f < n - 1) & (f - d >= 0))
        for d in range(n - 1, 1, -1):
            send(f + d, (f + d < n) & ((f >= half) | (f + d != half)))
            send(f - d, (f - d >= 0) & ((f < half) | (f - d != half - 1)))
        send(f - 1, f > half, pl.ds(cut, tokens - cut))
        send(f + 1, f + 1 < half, pl.ds(cut, tokens - cut))
        send(half, f < half - 1)
        send(half - 1, f > half)
        send(half - 1, f == half, pl.ds(cut, tokens - cut))
        send(half, f == half - 1, pl.ds(cut, tokens - cut))
        pltpu.make_async_copy(gis.at[f], share_of(gi, f, gis.shape[2]), own_s).start()
        gi_wait(n, f, gis, gi, gi_s, gi_r, own_s)


def settle_kernel(early, late, out, sem):
    s = lax.axis_index("section")
    at_once = lax.rem(s, 2) == AT_ONCE

    @pl.when(at_once)
    def _():
        copy = pltpu.make_async_copy(early, out, sem)
        copy.start()
        copy.wait()

    @pl.when(jnp.logical_not(at_once))
    def _():
        copy = pltpu.make_async_copy(late, out, sem)
        copy.start()
        copy.wait()


def body(layer_input, next_cot, w_value, micro_ids):
    n = lax.axis_size("fsdp")
    ns = lax.axis_size("section")
    tokens, width = layer_input.shape[1:]
    share, columns = w_value.shape[1:]
    hbm, vmem = pl.BlockSpec(memory_space=pltpu.HBM), pl.BlockSpec(memory_space=pltpu.VMEM)
    anywhere = pl.BlockSpec(memory_space=pl.ANY)
    dma, regular = pltpu.SemaphoreType.DMA, pltpu.SemaphoreType.REGULAR
    shape = jax.ShapeDtypeStruct
    stay = functools.partial(pltpu.with_memory_space_constraint, memory_space=pltpu.HBM)
    near = functools.partial(pltpu.with_memory_space_constraint, memory_space=pltpu.VMEM)
    early, gis, inc, lix, ids = pl.pallas_call(
        functools.partial(kernel, n, ns),
        out_shape=(
            shape((tokens, width), jnp.bfloat16),
            shape((n, tokens, share), jnp.bfloat16),
            shape((n, tokens, columns), jnp.bfloat16),
            shape((n, tokens, share), jnp.bfloat16),
            shape((n, 8, 128), jnp.int32),
        ),
        in_specs=[hbm, hbm, hbm, pl.BlockSpec(memory_space=pltpu.SMEM)],
        out_specs=(anywhere, vmem, vmem, vmem, vmem),
        scratch_shapes=[
            pltpu.VMEM((share, columns), jnp.bfloat16),
            dma, dma, dma((n,)), dma((n,)), dma((n,)), dma((n,)), dma((n,)),
            dma((n,)), dma((n,)), dma((n,)), dma((n,)), dma((4,)),
            regular((n,)), regular((n,)), regular,
            pltpu.VMEM((min(HEAD, PIECES) * (tokens // PIECES), share), jnp.bfloat16),
        ],
        compiler_params=pltpu.CompilerParams(
            collective_id=0, has_side_effects=True, vmem_limit_bytes=40 * 2**20
        ),
    )(stay(layer_input[0]), stay(next_cot[0]), stay(w_value[0]), micro_ids)
    wide = shape((share, columns), jnp.float32)
    grad_sum, grad_square, token = pl.pallas_call(
        functools.partial(weight_kernel, n),
        out_shape=(wide, wide, shape((8, 128), jnp.float32)),
        in_specs=[vmem, vmem, vmem],
        out_specs=(hbm, hbm, vmem),
        scratch_shapes=[
            pltpu.VMEM((share, columns), jnp.float32),
            pltpu.VMEM((share, columns), jnp.float32),
            dma((2, share // min(TILE, share))),
        ],
        compiler_params=pltpu.CompilerParams(vmem_limit_bytes=16 * 2**20),
    )(inc, lix, ids)
    late = pl.pallas_call(
        functools.partial(late_kernel, n),
        out_shape=shape((tokens, width), jnp.bfloat16),
        in_specs=[vmem, anywhere],
        out_specs=anywhere,
        scratch_shapes=[dma((n,)), dma((n,)), dma, regular((n,)), regular((n,))],
        compiler_params=pltpu.CompilerParams(
            collective_id=1, has_side_effects=True, vmem_limit_bytes=40 * 2**20
        ),
    )(gis, token)
    grad_input = pl.pallas_call(
        settle_kernel,
        out_shape=shape((tokens, width), jnp.bfloat16),
        in_specs=[anywhere, anywhere],
        out_specs=hbm,
        scratch_shapes=[dma],
        compiler_params=pltpu.CompilerParams(vmem_limit_bytes=4 * 2**20),
    )(near(early), near(late))
    return (grad_input[None], grad_sum[None], grad_square[None])


def solution(mesh):
    spec = P("section", "fsdp", None)
    return jax.shard_map(
        body,
        mesh=mesh,
        in_specs=(spec, spec, spec, P("section", "fsdp")),
        out_specs=(spec, spec, spec),
        check_vma=False,
    )
```
